128 devices in a mesh: row: 16 (over y_hi, x, core), col: 8 (over y_lo, z).
Axes of the slice: x: 4, y: 4 (y_hi: 2, y_lo: 2; y = y_hi * 2 + y_lo), z: 4, core: 2. Of those that a mesh axis runs over, the one named last changes fastest.
Arguments:
- pair_activation: bfloat16 [1024, 1024, 128], P('row', 'col'), may hold values from -80 to 80
- target_distance_bins: int32 [1024, 1024], P('row', 'col'), may hold values from 0 to 63, as said below
- distogram_weight: bfloat16 [128, 64], replicated, may hold values from -2 to 2
- distogram_bias: float32 [64], replicated, may hold values from -0.25 to 0.25
- outer_pair_weight: bfloat16 [1024, 128], replicated, may hold values from -0.1875 to 0.1875
- stored_lhs_operand: bfloat16 [256, 32, 1024], P('row', None, 'col'), may hold values from -6 to 6
- stored_rhs_operand: bfloat16 [256, 32, 1024], P('row', None, 'col'), may hold values from -6 to 6
- left_projection_weight: bfloat16 [64, 32], replicated, may hold values from -0.75 to 0.75
- right_projection_weight: bfloat16 [64, 32], replicated, may hold values from -0.75 to 0.75
- outer_mean_norm_gain: float32 [64], replicated, may hold values from 0.25 to 1.75
- transition_norm_gain: float32 [64], replicated, may hold values from 0.25 to 1.75
- gate_weight: bfloat16 [64, 256], replicated, may hold values from -0.75 to 0.75
- up_weight: bfloat16 [64, 256], replicated, may hold values from -0.75 to 0.75
- down_weight: bfloat16 [256, 64], replicated, may hold values from -0.375 to 0.375
- side_stack_entry: bfloat16 [256, 64, 1024], P(('row', 'col')), may hold values from -6 to 6
- arriving_stack_derivative: bfloat16 [256, 64, 1024], P(('row', 'col')), may hold values from -4 to 4
Outputs:
- pair_activation_gradient: bfloat16 [1024, 1024, 128], P('row', 'col')
- alignment_gradient: bfloat16 [256, 64, 1024], P(('row', 'col'))
The draws below stay inside these ranges and needn't reach their ends.
Inputs may be any that keep to these rules, and one draw needn't show every extreme that they name: target_distance_bins[i, j] equals target_distance_bins[j, i].
All inputs are finite; a program needn't handle non-finite values.
Results may differ from the reference program's by a relative error of at most 0.0098.
Values may be sent and summed in bfloat16 or wider, within the bound.
A program may use at most 64 MiB of HBM per device.

```python
import jax
import jax.numpy as jnp
from jax import lax

PAIR = 128
SIDE_FEATURE_LEN = 64
COMPONENT_WIDTH = 32
BINS = 64
HID = 256
SPAN_POSITIONS = 1024
OUTER = 1024
ALIGNED_CHAINS = 256


def distance_matrix(key):
    gaussian = jax.random.truncated_normal(jax.random.fold_in(key, 11), -4.0, 4.0, (PAIR, BINS), jnp.float32)
    return gaussian * (2.5 / PAIR ** 0.5)


def mirrored_ints(key, salt_value, upper_bound):
    raw_ints = jax.random.randint(jax.random.fold_in(key, salt_value), (SPAN_POSITIONS, SPAN_POSITIONS), 0, upper_bound)
    return raw_ints + raw_ints.T


def draw_distogram_weight(key, part):
    return distance_matrix(key).astype(jnp.bfloat16)


def draw_target_distance_bins(key, part):
    return (mirrored_ints(key, 21, BINS) % BINS).astype(jnp.int32)


def draw_pair_activation(key, part):
    gaussian = jax.random.truncated_normal(jax.random.fold_in(key, 3), -6.0, 6.0, (SPAN_POSITIONS, SPAN_POSITIONS, PAIR), jnp.float32)
    return gaussian.astype(jnp.bfloat16)


def steps_of(own_key, shape, shards, smallest, top_value):
    gain, own = 1.0, jax.random.fold_in(own_key, 6)
    for dim, shards_of in shards:
        draws = jnp.exp(jax.random.uniform(jax.random.fold_in(own, dim), (shards_of,), jnp.float32, smallest / len(shards), top_value / len(shards)))
        gain = gain * jnp.repeat(draws, shape[dim] // shards_of).reshape([-1 if axis == dim else 1 for axis in range(len(shape))])
    return gain


def bell_draw(stream_key, dims, spread, reach, cuts=(), kind=jnp.bfloat16):
    entries = spread * jax.random.normal(stream_key, dims, jnp.float32)
    if cuts:
        entries = entries * steps_of(stream_key, dims, cuts, -0.22, 0.18)
    return jnp.clip(entries, -reach, reach).astype(kind)


def setup_inputs(seed: int = 0) -> dict:
    key_list = jax.random.split(jax.random.key(seed), 17)
    pair_activation = draw_pair_activation(jax.random.fold_in(key_list[16], 71), 0)
    target_distance_bins = draw_target_distance_bins(jax.random.fold_in(key_list[16], 71), 0)
    distogram_weight = draw_distogram_weight(jax.random.fold_in(key_list[16], 71), 0)
    distogram_bias = jnp.clip(jax.random.uniform(key_list[3], (BINS,), jnp.float32, -0.25, 0.25), -0.25, 0.25)
    outer_pair_weight = bell_draw(key_list[4], (OUTER, PAIR), OUTER ** -0.5, 0.1875)
    stored_lhs_operand = bell_draw(key_list[5], (ALIGNED_CHAINS, COMPONENT_WIDTH, SPAN_POSITIONS), 1.0, 6.0, ((0, 16), (2, 8)))
    stored_rhs_operand = bell_draw(key_list[6], (ALIGNED_CHAINS, COMPONENT_WIDTH, SPAN_POSITIONS), 1.0, 6.0, ((0, 16), (2, 8)))
    left_projection_weight = bell_draw(key_list[7], (SIDE_FEATURE_LEN, COMPONENT_WIDTH), SIDE_FEATURE_LEN ** -0.5, 0.75)
    right_projection_weight = bell_draw(key_list[8], (SIDE_FEATURE_LEN, COMPONENT_WIDTH), SIDE_FEATURE_LEN ** -0.5, 0.75)
    outer_mean_norm_gain = jnp.clip(1.0 + 0.15 * jax.random.normal(key_list[9], (SIDE_FEATURE_LEN,), jnp.float32), 0.25, 1.75)
    transition_norm_gain = jnp.clip(1.0 + 0.15 * jax.random.normal(key_list[10], (SIDE_FEATURE_LEN,), jnp.float32), 0.25, 1.75)
    gate_weight = bell_draw(key_list[11], (SIDE_FEATURE_LEN, HID), SIDE_FEATURE_LEN ** -0.5, 0.75)
    up_weight = bell_draw(key_list[12], (SIDE_FEATURE_LEN, HID), SIDE_FEATURE_LEN ** -0.5, 0.75)
    down_weight = bell_draw(key_list[13], (HID, SIDE_FEATURE_LEN), HID ** -0.5, 0.375)
    side_stack_entry = bell_draw(key_list[14], (ALIGNED_CHAINS, SIDE_FEATURE_LEN, SPAN_POSITIONS), 1.0, 6.0, ((0, 128),))
    arriving_stack_derivative = bell_draw(key_list[15], (ALIGNED_CHAINS, SIDE_FEATURE_LEN, SPAN_POSITIONS), 0.25, 4.0, ((0, 128),))
    return {"pair_activation": pair_activation, "target_distance_bins": target_distance_bins, "distogram_weight": distogram_weight, "distogram_bias": distogram_bias, "outer_pair_weight": outer_pair_weight, "stored_lhs_operand": stored_lhs_operand, "stored_rhs_operand": stored_rhs_operand, "left_projection_weight": left_projection_weight, "right_projection_weight": right_projection_weight, "outer_mean_norm_gain": outer_mean_norm_gain, "transition_norm_gain": transition_norm_gain, "gate_weight": gate_weight, "up_weight": up_weight, "down_weight": down_weight, "side_stack_entry": side_stack_entry, "arriving_stack_derivative": arriving_stack_derivative}


def rounded(tensor):
    return lax.optimization_barrier(tensor.astype(jnp.bfloat16)).astype(jnp.float32)

def apply_layer_norm(features):
    centered = features - lax.optimization_barrier(jnp.mean(features, axis=1, keepdims=True))
    scale_inv = lax.rsqrt(lax.optimization_barrier(jnp.mean(centered * centered, axis=1, keepdims=True)) + 1e-05)
    return (centered * scale_inv, scale_inv)

def norm_backward_step(incoming, normed_field, scale_inv):
    first_mean = lax.optimization_barrier(jnp.mean(incoming, axis=1, keepdims=True))
    second_mean = lax.optimization_barrier(jnp.mean(incoming * normed_field, axis=1, keepdims=True))
    return scale_inv * (incoming - first_mean - normed_field * second_mean)

def reference(pair_activation, target_distance_bins, distogram_weight, distogram_bias, outer_pair_weight, stored_lhs_operand, stored_rhs_operand, left_projection_weight, right_projection_weight, outer_mean_norm_gain, transition_norm_gain, gate_weight, up_weight, down_weight, side_stack_entry, arriving_stack_derivative):
    dist_full = distogram_weight.astype(jnp.float32)
    logits = jnp.einsum('ijp,pb->bij', pair_activation.astype(jnp.float32), dist_full) + distogram_bias[:, None, None]
    logits = rounded(logits)
    symmetric = logits + jnp.swapaxes(logits, 1, 2)
    probability = jax.nn.softmax(symmetric, axis=0)
    bin_levels = jnp.arange(BINS, dtype=jnp.int32)[:, None, None]
    one_hot = (target_distance_bins[None, :, :] == bin_levels).astype(jnp.float32)
    logit_grad = rounded(2.0 * (probability - one_hot))
    pair_activation_gradient = jnp.einsum('bij,pb->ijp', logit_grad, dist_full).astype(jnp.bfloat16)
    outer_full = outer_pair_weight.astype(jnp.float32)
    left_full = stored_lhs_operand.astype(jnp.float32)
    rhs_complete = stored_rhs_operand.astype(jnp.float32)
    block_rows = 32
    tile_number = SPAN_POSITIONS // block_rows

    def single_tile(right_sum, block_index):
        row_start = block_index * block_rows
        grad_rows = lax.dynamic_slice_in_dim(pair_activation_gradient, row_start, block_rows, 0).astype(jnp.float32)
        tensor_product_derivative = rounded(jnp.einsum('ijp,kp->ijk', grad_rows, outer_full))
        tensor_product_derivative = tensor_product_derivative.reshape(block_rows, SPAN_POSITIONS, COMPONENT_WIDTH, COMPONENT_WIDTH)
        lhs_lines = lax.dynamic_slice_in_dim(left_full, row_start, block_rows, 2)
        lhs_portion = jnp.einsum('tdpa,wad->wpt', tensor_product_derivative, rhs_complete) / ALIGNED_CHAINS
        rhs_portion = jnp.einsum('doyw,vyd->vwo', tensor_product_derivative, lhs_lines) / ALIGNED_CHAINS
        return (right_sum + rhs_portion, lhs_portion)
    rhs_derivative, lhs_tiles = lax.scan(single_tile, jnp.zeros((ALIGNED_CHAINS, COMPONENT_WIDTH, SPAN_POSITIONS), jnp.float32), jnp.arange(tile_number, dtype=jnp.int32))
    lhs_derivative = jnp.transpose(lhs_tiles, (1, 2, 0, 3)).reshape(ALIGNED_CHAINS, COMPONENT_WIDTH, SPAN_POSITIONS)
    norm_input_gradient = jnp.einsum('mc,sci->smi', left_projection_weight.astype(jnp.float32), lhs_derivative, precision=lax.Precision.HIGHEST)
    norm_input_gradient = norm_input_gradient + jnp.einsum('me,sei->smi', right_projection_weight.astype(jnp.float32), rhs_derivative, precision=lax.Precision.HIGHEST)
    norm_input_gradient = rounded(norm_input_gradient)
    alignment_widened = side_stack_entry.astype(jnp.float32)
    first_normed_rows, first_inverse_scale = apply_layer_norm(alignment_widened)
    normed_input = rounded(first_normed_rows * transition_norm_gain[None, :, None])
    gate_value = jnp.einsum('smi,mh->shi', normed_input, gate_weight.astype(jnp.float32))
    upward = jnp.einsum('smi,mh->shi', normed_input, up_weight.astype(jnp.float32))
    hidden_state = rounded(jax.nn.silu(gate_value) * upward)
    alignment_output = alignment_widened + jnp.einsum('ajc,jr->arc', hidden_state, down_weight.astype(jnp.float32))
    second_normed_rows, second_inverse_scale = apply_layer_norm(alignment_output)
    middle_gradient = arriving_stack_derivative.astype(jnp.float32) + norm_backward_step(norm_input_gradient * outer_mean_norm_gain[None, :, None], second_normed_rows, second_inverse_scale)
    mid_half = rounded(middle_gradient)
    hidden_grad = jnp.einsum('smi,hm->shi', mid_half, down_weight.astype(jnp.float32))
    sigmoid_gate = jax.nn.sigmoid(gate_value)
    gate_grad = rounded(hidden_grad * upward * sigmoid_gate * (1.0 + gate_value * (1.0 - sigmoid_gate)))
    up_grad = rounded(hidden_grad * gate_value * sigmoid_gate)
    normed_rows_gradient = jnp.einsum('shi,mh->smi', gate_grad, gate_weight.astype(jnp.float32))
    normed_rows_gradient = normed_rows_gradient + jnp.einsum('shi,mh->smi', up_grad, up_weight.astype(jnp.float32))
    alignment_gradient = middle_gradient + norm_backward_step(normed_rows_gradient * transition_norm_gain[None, :, None], first_normed_rows, first_inverse_scale)
    return (pair_activation_gradient, alignment_gradient.astype(jnp.bfloat16))
```

```python
import functools

import jax
import jax.numpy as jnp
from jax import lax
from jax.experimental import pallas as pl
from jax.experimental.pallas import tpu as pltpu
from jax.sharding import PartitionSpec as P

MESH = pl.DeviceIdType.MESH
BF = jnp.bfloat16
F32 = jnp.float32
VM = pl.BlockSpec(memory_space=pltpu.VMEM)


def dot_nt(a, b):
    return lax.dot_general(a, b, (((1,), (1,)), ((), ())), preferred_element_type=F32)


def dot_nn(a, b):
    return lax.dot_general(a, b, (((1,), (0,)), ((), ())), preferred_element_type=F32)


def place():
    row, col = lax.axis_index("row"), lax.axis_index("col")
    return row, col, row // 8, (row // 2) % 4, row % 2, col // 4, col % 4


def full_barrier(row, col):
    barrier = pltpu.get_barrier_semaphore()
    me = row * 8 + col

    def greet(step, _):
        other = (me + step) % 128
        pl.semaphore_signal(
            barrier, inc=1, device_id={"row": other // 8, "col": other % 8}, device_id_type=MESH
        )
        return 0

    lax.fori_loop(1, 128, greet, 0)
    pl.semaphore_wait(barrier, 127)


def remote(src, dst, send, recv, row, col):
    return pltpu.make_async_remote_copy(
        src, dst, send, recv, device_id={"row": row, "col": col}, device_id_type=MESH
    )


def pair_index(pos):
    block, m = pos // 4, pos % 4
    return 2 * block + m % 2 + 16 * (m // 2)


def bias_columns(bias_ref):
    return jnp.broadcast_to(bias_ref[...], (128, 64)).T


def front_kernel(
    a_ref, tgt_ref, wd_ref, bias_ref, lhs_ref, rhs_ref, lg_ref, lrg_ref,
    a32, t_buf, b_buf, ra_buf, rb_buf, s32, loc_sem, m_send, m_recv, ra_send, ra_recv, rb_send, rb_recv,
    g_send, g_recv, p_send, p_recv,
):
    row, col, yh, x, k, yl, z = place()
    chip = row // 2
    full_barrier(row, col)
    mine = pl.ds(pl.multiple_of(row * 16, 16), 16)
    for side, ref in ((0, lhs_ref), (1, rhs_ref)):
        for s in range(16):
            s32[pl.ds(s * 32, 32), :] = ref[s].astype(F32)
        for e in range(32):
            lrg_ref[side, mine, e * 128 : (e + 1) * 128] = s32[pl.ds(e, 16, stride=32), :].astype(BF)
    wdt = wd_ref[...].astype(F32).T.astype(BF)
    bias = bias_columns(bias_ref)

    @pl.loop(0, 64)
    def _(i):
        a32[pl.ds(pl.multiple_of(i * 128, 128), 128), :] = a_ref[i].astype(F32)

    diag = x == z
    same_y = yh == yl
    sends = []
    for q in range(4):
        for kk in range(2):

            @pl.loop(0, 8)
            def _(p):
                ii = pair_index(q * 8 + p) + 64 * kk
                first = a32[pl.ds(ii + 32 * k, 64, stride=128), :]
                second = a32[pl.ds(ii + 32 * (1 - k), 64, stride=128), :]
                both = jnp.concatenate([first, second], axis=0).astype(BF)
                t_buf[kk, q, p] = (dot_nt(wdt, both) + bias).astype(BF)

            src = t_buf.at[kk, q]
            final = remote(src, b_buf.at[k, q], m_send.at[kk, q], m_recv.at[k, q], 2 * col + kk, chip)
            local = pltpu.make_async_copy(src, b_buf.at[k, q], loc_sem.at[q])
            home = jnp.logical_and(diag, same_y)
            own = jnp.logical_and(home, k == kk)
            if q % 2 == 0:
                direct = jnp.logical_and(jnp.logical_or(diag, same_y), jnp.logical_not(own))
                hop = remote(
                    src, ra_buf.at[kk, q // 2], m_send.at[kk, q], ra_recv.at[kk, q // 2],
                    yl * 8 + x * 2 + k, yh * 4 + z,
                )
            else:
                direct = jnp.logical_and(diag, jnp.logical_not(own))
                slot = (z - x + 3) % 4
                hop = remote(
                    src, rb_buf.at[slot, kk, q // 2], m_send.at[kk, q], rb_recv.at[slot, kk, q // 2],
                    yl * 8 + x * 2 + k, yh * 4 + x,
                )
            relayed = jnp.logical_not(jnp.logical_or(direct, own))
            pl.when(own)(local.start)
            pl.when(direct)(final.start)
            pl.when(relayed)(hop.start)
            sends.append((own, local, final))
    partner = row + 1 - 2 * k
    g_copies = []
    for step in range(1, 8):
        there = (row + 2 * step) % 16
        cp = remote(
            lrg_ref.at[:, mine], lrg_ref.at[:, mine], g_send.at[step], g_recv.at[step], there, col
        )
        cp.start()
        g_copies.append(cp)
    cp = remote(lrg_ref.at[:, mine], lrg_ref.at[:, mine], p_send.at[0], p_recv.at[0], partner, col)
    cp.start()
    p_copies = [cp]
    relay_a = jnp.logical_not(jnp.logical_or(diag, same_y))
    fa, fb = [], []
    for j in range(2):
        for kk in range(2):
            cp = remote(
                ra_buf.at[kk, j], b_buf.at[k, 2 * j], ra_send.at[kk, j], m_recv.at[k, 2 * j],
                2 * (yh * 4 + z) + kk, yl * 4 + x,
            )

            @pl.when(relay_a)
            def _():
                remote(
                    ra_buf.at[kk, j], ra_buf.at[kk, j], ra_send.at[kk, j], ra_recv.at[kk, j], row, col
                ).wait_recv()
                cp.start()

            fa.append(cp)
            for slot in range(3):
                zs = (x + 1 + slot) % 4
                cp2 = remote(
                    rb_buf.at[slot, kk, j], b_buf.at[k, 2 * j + 1], rb_send.at[slot, kk, j],
                    m_recv.at[k, 2 * j + 1], 2 * (yh * 4 + zs) + kk, yl * 4 + x,
                )

                @pl.when(diag)
                def _():
                    remote(
                        rb_buf.at[slot, kk, j], rb_buf.at[slot, kk, j], rb_send.at[slot, kk, j],
                        rb_recv.at[slot, kk, j], row, col,
                    ).wait_recv()
                    cp2.start()

                fb.append(cp2)
    lane = lax.broadcasted_iota(jnp.int32, (64, 128), 1)
    level = lax.broadcasted_iota(jnp.int32, (64, 128), 0)
    low = lane < 64
    home = jnp.logical_and(diag, same_y)
    for q in range(4):
        for kk in range(2):
            own = jnp.logical_and(home, k == kk)

            @pl.when(jnp.logical_not(own))
            def _():
                remote(
                    t_buf.at[0, q], b_buf.at[kk, q], m_send.at[0, q], m_recv.at[kk, q], row, col
                ).wait_recv()

            @pl.when(own)
            def _():
                pltpu.make_async_copy(t_buf.at[kk, q], b_buf.at[kk, q], loc_sem.at[q]).wait()

        @pl.loop(0, 8)
        def _(p):
            pos = q * 8 + p
            ii = pair_index(pos)
            b0 = b_buf[0, q, p].astype(F32)
            b1 = b_buf[1, q, p].astype(F32)
            mirrored = (
                jnp.where(low, b0, b1),
                pltpu.roll(jnp.where(low, b1, b0), 64, 1),
            )
            for h in range(2):
                i = ii + 32 * h
                own_logits = (dot_nt(wdt, a_ref[i]) + bias).astype(BF).astype(F32)
                sym = own_logits + mirrored[h]
                top = jnp.max(sym, axis=0, keepdims=True)
                ex = jnp.exp(sym - top)
                prob = ex / jnp.sum(ex, axis=0, keepdims=True)
                tgt = tgt_ref[pl.ds(i, 1), :]
                hot = jnp.where(level == tgt, 1.0, 0.0)
                lg_ref[pos, h] = (2.0 * (prob - hot)).astype(BF)

    for step in range(1, 8):
        source = (row - 2 * step + 16) % 16
        rows = pl.ds(pl.multiple_of(source * 16, 16), 16)
        remote(
            lrg_ref.at[:, rows], lrg_ref.at[:, rows], g_send.at[step], g_recv.at[step], row, col
        ).wait_recv()
        cp = remote(
            lrg_ref.at[:, rows], lrg_ref.at[:, rows], p_send.at[step], p_recv.at[step], partner, col
        )
        cp.start()
        p_copies.append(cp)
    for step in range(8):
        source = (partner - 2 * step + 16) % 16
        rows = pl.ds(pl.multiple_of(source * 16, 16), 16)
        remote(
            lrg_ref.at[:, rows], lrg_ref.at[:, rows], p_send.at[step], p_recv.at[step], row, col
        ).wait_recv()
    for cp in g_copies + p_copies:
        cp.wait_send()
    for own, local, final in sends:
        pl.when(jnp.logical_not(own))(final.wait_send)
    for cp in fa:
        pl.when(relay_a)(cp.wait_send)
    for cp in fb:
        pl.when(diag)(cp.wait_send)


def front(a, tgt, wd, bias, lhs, rhs):
    dma = pltpu.SemaphoreType.DMA
    return pl.pallas_call(
        front_kernel,
        out_shape=(
            jax.ShapeDtypeStruct((32, 2, 64, 128), BF),
            jax.ShapeDtypeStruct((2, 256, 4096), BF),
        ),
        in_specs=[VM] * 6,
        out_specs=(VM, VM),
        scratch_shapes=[
            pltpu.VMEM((8192, 128), F32),
            pltpu.VMEM((2, 4, 8, 64, 128), BF),
            pltpu.VMEM((2, 4, 8, 64, 128), BF),
            pltpu.VMEM((2, 2, 8, 64, 128), BF),
            pltpu.VMEM((3, 2, 2, 8, 64, 128), BF),
            pltpu.VMEM((512, 128), F32),
            dma((4,)),
            dma((2, 4)),
            dma((2, 4)),
            dma((2, 2)),
            dma((2, 2)),
            dma((3, 2, 2)),
            dma((3, 2, 2)),
            dma((8,)),
            dma((8,)),
            dma((8,)),
            dma((8,)),
        ],
        compiler_params=pltpu.CompilerParams(
            collective_id=0, has_side_effects=True, vmem_limit_bytes=60 << 20
        ),
        name="front",
    )(a, tgt, wd, bias, lhs, rhs)


def middle_kernel(lg_ref, lrg_ref, wd_ref, wo_ref, g_ref, part_ref, w32, wec, xs, o32):
    wd = wd_ref[...]
    wdt = wd.astype(F32).T.astype(BF)
    w32[...] = wo_ref[...].astype(F32)
    for e in range(32):
        wec[pl.ds(e * 32, 32), :] = w32[pl.ds(e, 32, stride=32), :].astype(BF)

    @pl.loop(0, 8)
    def _(block):
        @pl.loop(0, 4)
        def _(m):
            pos = block * 4 + m
            ii = pair_index(pos)
            pair = jnp.concatenate([lg_ref[pos, 0], lg_ref[pos, 1]], axis=1)
            gt = dot_nn(wd, pair).astype(BF)
            for h in range(2):
                lgt = lg_ref[pos, h].astype(F32).T.astype(BF)
                g_ref[ii + 32 * h] = dot_nn(lgt, wdt).astype(BF)
            for side, w in ((0, wec), (1, wo_ref)):
                for n in range(4):
                    u = dot_nn(w[pl.ds(n * 256, 256), :], gt).astype(BF)
                    for h in range(2):
                        base = pl.multiple_of((m % 2) * 128 + (m // 2) * 32 + 64 * h, 32)
                        for f in range(8):
                            e = n * 8 + f
                            xs[side, pl.ds(base, 32), e * 128 : (e + 1) * 128] = u[
                                f * 32 : (f + 1) * 32, h * 128 : (h + 1) * 128
                            ]

        for side in range(2):
            out = dot_nt(lrg_ref[1 - side], xs[side])
            for half in range(2):
                o32[...] = out[:, half * 128 : (half + 1) * 128]
                for w in range(16):
                    part_ref[w // 2, block, side, half, (w % 2) * 16 : (w % 2) * 16 + 16, :] = o32[
                        pl.ds(w, 16, stride=16), :
                    ].astype(BF)


def middle(lg, lrg, wd, wo):
    return pl.pallas_call(
        middle_kernel,
        out_shape=(
            jax.ShapeDtypeStruct((64, 128, 128), BF),
            jax.ShapeDtypeStruct((8, 8, 2, 2, 32, 128), BF),
        ),
        in_specs=[VM] * 4,
        out_specs=(VM, VM),
        scratch_shapes=[
            pltpu.VMEM((1024, 128), F32),
            pltpu.VMEM((1024, 128), BF),
            pltpu.VMEM((2, 256, 4096), BF),
            pltpu.VMEM((256, 128), F32),
        ],
        compiler_params=pltpu.CompilerParams(vmem_limit_bytes=60 << 20),
        name="middle",
    )(lg, lrg, wd, wo)


def reduce_kernel(part_ref, fin_ref, got, s32, s16, r_send, r_recv, a_send, a_recv):
    row, col, yh, x, k, yl, z = place()
    full_barrier(row, col)
    copies = []
    for step in range(1, 8):
        there = (col + step) % 8
        cp = remote(
            part_ref.at[there], got.at[step - 1], r_send.at[step - 1], r_recv.at[step - 1], row, there
        )
        cp.start()
        copies.append(cp)
    for cp in copies:
        cp.wait_recv()

    @pl.loop(0, 8)
    def _(block):
        for side in range(2):
            for half in range(2):
                total = part_ref[col, block, side, half].astype(F32)
                for step in range(7):
                    total += got[step, block, side, half].astype(F32)
                q = side * 16 + block * 2 + half
                for t in range(2):
                    s32[pl.ds(t * 32 + q, 16, stride=64), :] = total[t * 16 : (t + 1) * 16]

    for there in range(16):
        s16[there] = s32[pl.ds(there * 64, 64), :].astype(BF)
    fin_ref[row] = s16[row]
    for step in range(1, 16):
        there = (row + step) % 16
        cp = remote(s16.at[there], fin_ref.at[row], a_send.at[step], a_recv.at[step], there, col)
        cp.start()
        copies.append(cp)
    for step in range(1, 16):
        source = (row - step + 16) % 16
        remote(
            s16.at[0], fin_ref.at[source], a_send.at[step], a_recv.at[step], row, col
        ).wait_recv()
    for cp in copies:
        cp.wait_send()


def reduce(part):
    dma = pltpu.SemaphoreType.DMA
    return pl.pallas_call(
        reduce_kernel,
        out_shape=jax.ShapeDtypeStruct((16, 64, 128), BF),
        in_specs=[VM],
        out_specs=VM,
        scratch_shapes=[
            pltpu.VMEM((7, 8, 2, 2, 32, 128), BF),
            pltpu.VMEM((1024, 128), F32),
            pltpu.VMEM((16, 64, 128), BF),
            dma((7,)),
            dma((7,)),
            dma((16,)),
            dma((16,)),
        ],
        compiler_params=pltpu.CompilerParams(
            collective_id=1, has_side_effects=True, vmem_limit_bytes=60 << 20
        ),
        name="reduce",
    )(part)


def norm_forward(v):
    centered = v - jnp.mean(v, axis=0, keepdims=True)
    inv = lax.rsqrt(jnp.mean(centered * centered, axis=0, keepdims=True) + 1e-05)
    return centered * inv, inv


def norm_backward(g, normed, inv):
    first = jnp.mean(g, axis=0, keepdims=True)
    second = jnp.mean(g * normed, axis=0, keepdims=True)
    return inv * (g - first - normed * second)


def column(ref):
    return jnp.broadcast_to(ref[...], (128, ref.shape[1])).T[:, :1]


def tail_kernel(
    fin_ref, side_ref, arrive_ref, lw_ref, rw_ref, og_ref, tg_ref, gw_ref, uw_ref, dw_ref, out_ref, wts
):
    lanes = 256
    gwt = gw_ref[...].astype(F32).T.astype(BF)
    uwt = uw_ref[...].astype(F32).T.astype(BF)
    dwt = dw_ref[...].astype(F32).T.astype(BF)
    gw, uw, dw = gw_ref[...], uw_ref[...], dw_ref[...]
    lw, rw = lw_ref[...], rw_ref[...]
    ab = jnp.concatenate([lw] * 4 + [rw] * 4, axis=1)
    og, tg = column(og_ref), column(tg_ref)
    group = lax.broadcasted_iota(jnp.int32, (16, 128), 1) // 32
    zero = jnp.zeros((16, 128), BF)

    @pl.loop(0, 2)
    def _(s):
        @pl.loop(0, 1024 // lanes)
        def _(n):
            for r in range(lanes // 64):
                for side in range(2):
                    rows = fin_ref[n * (lanes // 64) + r, pl.ds(pl.multiple_of(s * 32 + side * 16, 16), 16), :]
                    for lo in range(4):
                        wts[pl.ds(r * 64 + lo * 16, 16), side * 128 : side * 128 + 128] = jnp.where(
                            group == lo, rows, zero
                        )
            at = pl.ds(pl.multiple_of(n * lanes, lanes), lanes)
            ng = (dot_nt(ab, wts[...]) * (1.0 / 256)).astype(BF).astype(F32)
            v = side_ref[s, :, at].astype(F32)
            n1, inv1 = norm_forward(v)
            nin = (n1 * tg).astype(BF)
            gate = dot_nn(gwt, nin)
            up = dot_nn(uwt, nin)
            sig = jax.nn.sigmoid(gate)
            act = gate * sig
            hidden = (act * up).astype(BF)
            n2, inv2 = norm_forward(v + dot_nn(dwt, hidden))
            mid = arrive_ref[s, :, at].astype(F32) + norm_backward(ng * og, n2, inv2)
            hg = dot_nn(dw, mid.astype(BF))
            gg = (hg * up * sig * (1.0 + gate * (1.0 - sig))).astype(BF)
            ug = (hg * act).astype(BF)
            nrg = dot_nn(gw, gg) + dot_nn(uw, ug)
            out_ref[s, :, at] = (mid + norm_backward(nrg * tg, n1, inv1)).astype(BF)


def tail(fin, side, arrive, lw, rw, og, tg, gw, uw, dw):
    return pl.pallas_call(
        tail_kernel,
        out_shape=jax.ShapeDtypeStruct((2, 64, 1024), BF),
        in_specs=[VM] * 10,
        out_specs=VM,
        scratch_shapes=[pltpu.VMEM((256, 256), BF)],
        compiler_params=pltpu.CompilerParams(vmem_limit_bytes=40 << 20),
        name="tail",
    )(fin, side, arrive, lw, rw, og, tg, gw, uw, dw)


def per_device(
    pair_activation, target_distance_bins, distogram_weight, distogram_bias, outer_pair_weight,
    stored_lhs_operand, stored_rhs_operand, left_projection_weight, right_projection_weight,
    outer_mean_norm_gain, transition_norm_gain, gate_weight, up_weight, down_weight,
    side_stack_entry, arriving_stack_derivative,
):
    lg, lrg = front(
        pair_activation, target_distance_bins, distogram_weight, distogram_bias.reshape(1, -1),
        stored_lhs_operand, stored_rhs_operand,
    )
    g, part = middle(lg, lrg, distogram_weight, outer_pair_weight)
    fin = reduce(part)
    out = tail(
        fin, side_stack_entry, arriving_stack_derivative, left_projection_weight,
        right_projection_weight, outer_mean_norm_gain.reshape(1, -1),
        transition_norm_gain.reshape(1, -1), gate_weight, up_weight, down_weight,
    )
    return g, out


def solution(mesh):
    return jax.shard_map(
        per_device,
        mesh=mesh,
        in_specs=(
            P("row", "col", None),
            P("row", "col"),
            P(),
            P(),
            P(),
            P("row", None, "col"),
            P("row", None, "col"),
            P(),
            P(),
            P(),
            P(),
            P(),
            P(),
            P(),
            P(("row", "col"), None, None),
            P(("row", "col"), None, None),
        ),
        out_specs=(P("row", "col", None), P(("row", "col"), None, None)),
        check_vma=False,
    )
```

```python
import functools

import jax
import jax.numpy as jnp
from jax import lax
from jax.experimental import pallas as pl
from jax.experimental.pallas import tpu as pltpu
from jax.sharding import PartitionSpec as P

MESH = pl.DeviceIdType.MESH
BF = jnp.bfloat16
F32 = jnp.float32
VM = pl.BlockSpec(memory_space=pltpu.VMEM)


def dot_nt(a, b):
    return lax.dot_general(a, b, (((1,), (1,)), ((), ())), preferred_element_type=F32)


def dot_nn(a, b):
    return lax.dot_general(a, b, (((1,), (0,)), ((), ())), preferred_element_type=F32)


def place():
    row, col = lax.axis_index("row"), lax.axis_index("col")
    return row, col, row // 8, (row // 2) % 4, row % 2, col // 4, col % 4


def full_barrier(row, col):
    barrier = pltpu.get_barrier_semaphore()
    me = row * 8 + col

    def greet(step, _):
        other = (me + step) % 128
        pl.semaphore_signal(
            barrier, inc=1, device_id={"row": other // 8, "col": other % 8}, device_id_type=MESH
        )
        return 0

    lax.fori_loop(1, 128, greet, 0)
    pl.semaphore_wait(barrier, 127)


def remote(src, dst, send, recv, row, col):
    return pltpu.make_async_remote_copy(
        src, dst, send, recv, device_id={"row": row, "col": col}, device_id_type=MESH
    )


def pair_index(pos):
    block, m = pos // 4, pos % 4
    return 2 * block + m % 2 + 16 * (m // 2)


def bias_columns(bias_ref):
    return jnp.broadcast_to(bias_ref[...], (128, 64)).T


def arrived(dst, recv, row, col):
    remote(dst, dst, recv, recv, row, col).wait_recv()


BLOCK_Y = (True, False, True, False, True, False, True, True)


def main_kernel(
    a_ref, tgt_ref, wd_ref, bias_ref, wo_ref, lhs_ref, rhs_ref, g_hbm, fin_ref,
    a32, t_buf, b_buf, ra_buf, rb_buf, s32, lrg, g_buf, w32, wec, xs, o32, part, got_y, got_z, fin32, fin16, own_buf, gt_buf,
    loc_sem, m_send, m_recv, ra_send, ra_recv, rb_send, rb_recv,
    gx_send, gx_recv, p_send, p_recv, out_sem, y_send, y_recv, z_send, z_recv, f_send, f_recv,
):
    row, col, yh, x, k, yl, z = place()
    chip = row // 2
    diag = x == z
    same_y = yh == yl
    home = jnp.logical_and(diag, same_y)
    partner = row + 1 - 2 * k
    sends = []

    def go(cp, when=None):
        if when is None:
            cp.start()
        else:
            pl.when(when)(cp.start)
        sends.append((cp, when))

    def block_rows(r):
        return pl.ds(pl.multiple_of(r * 16, 16), 16)

    def x_row(r, d):
        return (r // 8) * 8 + (((r // 2) % 4 + d) % 4) * 2 + r % 2

    full_barrier(row, col)
    mine = block_rows(row)
    for side, ref in ((0, lhs_ref), (1, rhs_ref)):
        for s in range(16):
            s32[pl.ds(s * 32, 32), :] = ref[s].astype(F32)
        for e in range(32):
            lrg[side, mine, e * 128 : (e + 1) * 128] = s32[pl.ds(e, 16, stride=32), :].astype(BF)

    def whole(r):
        return lrg.at[:, block_rows(r)]

    def share(r, slot):
        go(remote(whole(r), whole(r), p_send.at[slot], p_recv.at[slot], partner, col))

    def gather_send(r, slot, there, side=None):
        ref = whole(r) if side is None else lrg.at[side, block_rows(r)]
        go(remote(ref, ref, gx_send.at[slot], gx_recv.at[slot], there, col))

    def gather_wait(r, slot, side=None):
        ref = whole(r) if side is None else lrg.at[side, block_rows(r)]
        arrived(ref, gx_recv.at[slot], row, col)

    flip = (row + 8) % 16
    left, right = x_row(row, 3), x_row(row, 1)
    flip_left, flip_right = x_row(flip, 3), x_row(flip, 1)
    far, flip_far = x_row(row, 2), x_row(flip, 2)
    gather_send(row, 0, flip)
    gather_send(row, 1, right)
    gather_send(row, 2, left)
    share(row, 0)

    wdt = wd_ref[...]
    wd = wdt.astype(F32).T.astype(BF)
    bias = bias_columns(bias_ref)

    @pl.loop(0, 64, unroll=4)
    def _(i):
        a32[pl.ds(pl.multiple_of(i * 128, 128), 128), :] = a_ref[i].astype(F32)

    for q in range(4):
        for kk in range(2):

            @pl.loop(0, 8, unroll=8)
            def _(p):
                ii = pair_index(q * 8 + p) + 64 * kk
                first = a32[pl.ds(ii + 32 * k, 64, stride=128), :]
                second = a32[pl.ds(ii + 32 * (1 - k), 64, stride=128), :]
                both = jnp.concatenate([first, second], axis=0).astype(BF)
                t_buf[kk, q, p] = (dot_nt(wdt, both) + bias).astype(BF)

            src = t_buf.at[kk, q]
            final = remote(src, b_buf.at[k, q], m_send.at[kk, q], m_recv.at[k, q], 2 * col + kk, chip)
            local = pltpu.make_async_copy(src, b_buf.at[k, q], loc_sem.at[q])
            own = jnp.logical_and(home, k == kk)
            if q % 2 == 0:
                direct = jnp.logical_and(jnp.logical_or(diag, same_y), jnp.logical_not(own))
                hop = remote(
                    src, ra_buf.at[kk, q // 2], m_send.at[kk, q], ra_recv.at[kk, q // 2],
                    yl * 8 + x * 2 + k, yh * 4 + z,
                )
            else:
                direct = jnp.logical_and(diag, jnp.logical_not(own))
                slot = (z - x + 3) % 4
                hop = remote(
                    src, rb_buf.at[slot, kk, q // 2], m_send.at[kk, q], rb_recv.at[slot, kk, q // 2],
                    yl * 8 + x * 2 + k, yh * 4 + x,
                )
            relayed = jnp.logical_not(jnp.logical_or(direct, own))
            pl.when(own)(local.start)
            pl.when(direct)(final.start)
            pl.when(relayed)(hop.start)
            sends.append((final, jnp.logical_not(own)))

    w32[...] = wo_ref[...].astype(F32)
    for e in range(32):
        wec[pl.ds(e * 32, 32), :] = w32[pl.ds(e, 32, stride=32), :].astype(BF)

    gather_wait(flip, 0)
    gather_send(flip, 3, right)
    gather_send(flip, 4, left)
    share(flip, 1)

    relay_a = jnp.logical_not(jnp.logical_or(diag, same_y))

    def relay(j):
        for kk in range(2):
            pl.when(relay_a)(functools.partial(arrived, ra_buf.at[kk, j], ra_recv.at[kk, j], row, col))
            go(
                remote(
                    ra_buf.at[kk, j], b_buf.at[k, 2 * j], ra_send.at[kk, j], m_recv.at[k, 2 * j],
                    2 * (yh * 4 + z) + kk, yl * 4 + x,
                ),
                relay_a,
            )
        for kk in range(2):
            for slot in range(3):
                zs = (x + 1 + slot) % 4
                pl.when(diag)(
                    functools.partial(arrived, rb_buf.at[slot, kk, j], rb_recv.at[slot, kk, j], row, col)
                )
                go(
                    remote(
                        rb_buf.at[slot, kk, j], b_buf.at[k, 2 * j + 1], rb_send.at[slot, kk, j],
                        m_recv.at[k, 2 * j + 1], 2 * (yh * 4 + zs) + kk, yl * 4 + x,
                    ),
                    diag,
                )

    @pl.loop(0, 64, unroll=8)
    def _(i):
        own_buf[i] = (dot_nt(wdt, a_ref[i]) + bias).astype(BF)

    relay(0)
    relay(1)

    def pass_on(near_left, near_right, slots, shares):
        gather_wait(near_left, slots[0])
        gather_send(near_left, slots[2], right, 0)
        share(near_left, shares[0])
        gather_wait(near_right, slots[1])
        gather_send(near_right, slots[3], left, 1)
        share(near_right, shares[1])

    lane = lax.broadcasted_iota(jnp.int32, (64, 128), 1)
    level = lax.broadcasted_iota(jnp.int32, (64, 128), 0)
    low = lane < 64
    out_copies = []
    for q in range(4):
        for kk in range(2):
            own = jnp.logical_and(home, k == kk)
            pl.when(jnp.logical_not(own))(
                functools.partial(arrived, b_buf.at[kk, q], m_recv.at[kk, q], row, col)
            )
            pl.when(own)(pltpu.make_async_copy(t_buf.at[kk, q], b_buf.at[kk, q], loc_sem.at[q]).wait)

        @pl.loop(0, 8, unroll=4)
        def _(p):
            pos = q * 8 + p
            ii = pair_index(pos)
            b0 = b_buf[0, q, p].astype(F32)
            b1 = b_buf[1, q, p].astype(F32)
            mirrored = (
                jnp.where(low, b0, b1),
                pltpu.roll(jnp.where(low, b1, b0), 64, 1),
            )
            grads = []
            for h in range(2):
                i = ii + 32 * h
                sym = own_buf[i].astype(F32) + mirrored[h]
                top = jnp.max(sym, axis=0, keepdims=True)
                ex = jnp.exp(sym - top)
                prob = ex / jnp.sum(ex, axis=0, keepdims=True)
                tgt = tgt_ref[pl.ds(i, 1), :]
                hot = jnp.where(level == tgt, 1.0, 0.0)
                grad = 2.0 * (prob - hot)
                g_buf[i] = dot_nn(grad.T.astype(BF), wdt).astype(BF)
                grads.append(grad.astype(BF))
            gt_buf[p] = dot_nn(wd, jnp.concatenate(grads, axis=1)).astype(BF)

        @pl.loop(0, 8, unroll=2)
        def _(p):
            pos = q * 8 + p
            block, m = pos // 4, pos % 4
            gt = gt_buf[p]
            for side, w in ((0, wec), (1, wo_ref)):
                for n in range(4):
                    u = dot_nn(w[pl.ds(n * 256, 256), :], gt).astype(BF)
                    for h in range(2):
                        base = pl.multiple_of((m % 2) * 128 + (m // 2) * 32 + 64 * h, 32)
                        for f in range(8):
                            e = n * 8 + f
                            xs[side, block, pl.ds(base, 32), e * 128 : (e + 1) * 128] = u[
                                f * 32 : (f + 1) * 32, h * 128 : (h + 1) * 128
                            ]

        for lo in range(4):
            rows = pl.ds(lo * 16 + 4 * q, 4)
            cp = pltpu.make_async_copy(g_buf.at[rows], g_hbm.at[rows], out_sem.at[q, lo])
            cp.start()
            out_copies.append(cp)
        if q == 1:
            pass_on(left, right, (1, 2, 5, 6), (2, 3))
        if q == 2:
            pass_on(flip_left, flip_right, (3, 4, 7, 8), (4, 5))

    for side, r, slot in ((0, far, 5), (1, far, 6), (0, flip_far, 7), (1, flip_far, 8)):
        gather_wait(r, slot, side)
    share(far, 6)
    share(flip_far, 7)
    for slot, r in enumerate((row, flip, left, right, flip_left, flip_right, far, flip_far)):
        r = r + 1 - 2 * k
        arrived(whole(r), p_recv.at[slot], row, col)

    other = (1 - yl) * 4
    home4 = pl.multiple_of(yl * 4, 4)

    def contract(block):
        for side in range(2):
            out = dot_nt(lrg[1 - side], xs[side, block])
            for half in range(2):
                o32[...] = out[:, half * 128 : (half + 1) * 128]
                for w in range(16):
                    part[block, w // 2, side, half, (w % 2) * 16 : (w % 2) * 16 + 16, :] = o32[
                        pl.ds(w, 16, stride=16), :
                    ].astype(BF)
        if BLOCK_Y[block]:
            go(
                remote(
                    part.at[block, pl.ds(other, 4)], got_y.at[block], y_send.at[block], y_recv.at[block],
                    row, other + z,
                )
            )
        else:
            for d in range(1, 4):
                zz = (z + d) % 4
                for y2 in range(2):
                    go(
                        remote(
                            part.at[block, y2 * 4 + zz], got_z.at[block, d - 1, y2],
                            z_send.at[block, d - 1, y2], z_recv.at[block, d - 1, y2], row, yl * 4 + zz,
                        )
                    )

    def second(block):
        if BLOCK_Y[block]:
            arrived(got_y.at[block], y_recv.at[block], row, col)

            @pl.loop(0, 4)
            def _(zz):
                for side in range(2):
                    for half in range(2):
                        part[block, home4 + zz, side, half] = (
                            part[block, home4 + zz, side, half].astype(F32)
                            + got_y[block, zz, side, half].astype(F32)
                        ).astype(BF)

            for d in range(1, 4):
                zz = (z + d) % 4
                go(
                    remote(
                        part.at[block, yl * 4 + zz], got_z.at[block, d - 1, 0],
                        z_send.at[block, d - 1, 0], z_recv.at[block, d - 1, 0], row, yl * 4 + zz,
                    )
                )
        else:
            for d in range(1, 4):
                for y2 in range(2):
                    arrived(got_z.at[block, d - 1, y2], z_recv.at[block, d - 1, y2], row, col)
            for y2 in range(2):
                for side in range(2):
                    for half in range(2):
                        total = part[block, y2 * 4 + z, side, half].astype(F32)
                        for d in range(3):
                            total += got_z[block, d, y2, side, half].astype(F32)
                        part[block, y2 * 4 + z, side, half] = total.astype(BF)
            go(
                remote(
                    part.at[block, other + z], got_y.at[block, 0], y_send.at[block], y_recv.at[block],
                    row, other + z,
                )
            )

    def third(block):
        if BLOCK_Y[block]:
            for d in range(1, 4):
                arrived(got_z.at[block, d - 1, 0], z_recv.at[block, d - 1, 0], row, col)
        else:
            arrived(got_y.at[block, 0], y_recv.at[block], row, col)
        for side in range(2):
            for half in range(2):
                total = part[block, col, side, half].astype(F32)
                if BLOCK_Y[block]:
                    for d in range(3):
                        total += got_z[block, d, 0, side, half].astype(F32)
                else:
                    total += got_y[block, 0, side, half].astype(F32)
                tile = side * 16 + block * 2 + half
                for t in range(2):
                    fin32[pl.ds(t * 32 + tile, 16, stride=64), :] = total[t * 16 : (t + 1) * 16]

    for block in range(8):
        contract(block)
        if block >= 2:
            second(block - 2)
        if block >= 5:
            third(block - 5)
    second(6)
    second(7)
    for block in range(3, 8):
        third(block)

    for there in range(16):
        fin16[there] = fin32[pl.ds(there * 64, 64), :].astype(BF)
    fin_ref[row] = fin16[row]
    for step in range(1, 16):
        there = (row + step) % 16
        go(remote(fin16.at[there], fin_ref.at[row], f_send.at[step], f_recv.at[step], there, col))
    for step in range(1, 16):
        source = (row - step + 16) % 16
        arrived(fin_ref.at[source], f_recv.at[step], row, col)
    for cp, when in sends:
        if when is None:
            cp.wait_send()
        else:
            pl.when(when)(cp.wait_send)
    for cp in out_copies:
        cp.wait()


def main(a, tgt, wd, bias, wo, lhs, rhs):
    dma = pltpu.SemaphoreType.DMA
    return pl.pallas_call(
        main_kernel,
        out_shape=(
            jax.ShapeDtypeStruct((64, 128, 128), BF),
            jax.ShapeDtypeStruct((16, 64, 128), BF),
        ),
        in_specs=[VM] * 7,
        out_specs=(pl.BlockSpec(memory_space=pl.ANY), VM),
        scratch_shapes=[
            pltpu.VMEM((8192, 128), F32),
            pltpu.VMEM((2, 4, 8, 64, 128), BF),
            pltpu.VMEM((2, 4, 8, 64, 128), BF),
            pltpu.VMEM((2, 2, 8, 64, 128), BF),
            pltpu.VMEM((3, 2, 2, 8, 64, 128), BF),
            pltpu.VMEM((512, 128), F32),
            pltpu.VMEM((2, 256, 4096), BF),
            pltpu.VMEM((64, 128, 128), BF),
            pltpu.VMEM((1024, 128), F32),
            pltpu.VMEM((1024, 128), BF),
            pltpu.VMEM((2, 8, 256, 4096), BF),
            pltpu.VMEM((256, 128), F32),
            pltpu.VMEM((8, 8, 2, 2, 32, 128), BF),
            pltpu.VMEM((8, 4, 2, 2, 32, 128), BF),
            pltpu.VMEM((8, 3, 2, 2, 2, 32, 128), BF),
            pltpu.VMEM((1024, 128), F32),
            pltpu.VMEM((16, 64, 128), BF),
            pltpu.VMEM((64, 64, 128), BF),
            pltpu.VMEM((8, 128, 256), BF),
            dma((4,)),
            dma((2, 4)),
            dma((2, 4)),
            dma((2, 2)),
            dma((2, 2)),
            dma((3, 2, 2)),
            dma((3, 2, 2)),
            dma((9,)),
            dma((9,)),
            dma((8,)),
            dma((8,)),
            dma((4, 4)),
            dma((8,)),
            dma((8,)),
            dma((8, 3, 2)),
            dma((8, 3, 2)),
            dma((16,)),
            dma((16,)),
        ],
        compiler_params=pltpu.CompilerParams(
            collective_id=0, has_side_effects=True, vmem_limit_bytes=67043328
        ),
        name="main",
    )(a, tgt, wd, bias, wo, lhs, rhs)


def norm_forward(v):
    centered = v - jnp.mean(v, axis=0, keepdims=True)
    inv = lax.rsqrt(jnp.mean(centered * centered, axis=0, keepdims=True) + 1e-05)
    return centered * inv, inv


def norm_backward(g, normed, inv):
    first = jnp.mean(g, axis=0, keepdims=True)
    second = jnp.mean(g * normed, axis=0, keepdims=True)
    return inv * (g - first - normed * second)


def column(ref):
    return jnp.broadcast_to(ref[...], (128, ref.shape[1])).T[:, :1]


def tail_kernel(
    g_in, fin_ref, side_ref, arrive_ref, lw_ref, rw_ref, og_ref, tg_ref, gw_ref, uw_ref, dw_ref, g_out, out_ref,
    wts, g_stage, g_sem,
):
    fetch = [
        pltpu.make_async_copy(g_in.at[pl.ds(n * 16, 16)], g_stage.at[pl.ds(n * 16, 16)], g_sem.at[0, n])
        for n in range(4)
    ]
    store = [
        pltpu.make_async_copy(g_stage.at[pl.ds(n * 16, 16)], g_out.at[pl.ds(n * 16, 16)], g_sem.at[1, n])
        for n in range(4)
    ]
    for cp in fetch:
        cp.start()
    for cp, back in zip(fetch, store):
        cp.wait()
        back.start()
    lanes = 256
    gwt = gw_ref[...].astype(F32).T.astype(BF)
    uwt = uw_ref[...].astype(F32).T.astype(BF)
    dwt = dw_ref[...]
    gw, uw, dw = gw_ref[...], uw_ref[...], dwt.astype(F32).T.astype(BF)
    lwt, rwt = lw_ref[...], rw_ref[...]
    ab = jnp.concatenate([lwt] * 4 + [rwt] * 4, axis=0).astype(F32).T.astype(BF)
    og, tg = column(og_ref), column(tg_ref)
    group = lax.broadcasted_iota(jnp.int32, (16, 128), 1) // 32
    zero = jnp.zeros((16, 128), BF)

    @pl.loop(0, 2)
    def _(s):
        @pl.loop(0, 1024 // lanes)
        def _(n):
            for r in range(lanes // 64):
                for side in range(2):
                    rows = fin_ref[n * (lanes // 64) + r, pl.ds(pl.multiple_of(s * 32 + side * 16, 16), 16), :]
                    for lo in range(4):
                        wts[pl.ds(r * 64 + lo * 16, 16), side * 128 : side * 128 + 128] = jnp.where(
                            group == lo, rows, zero
                        )
            at = pl.ds(pl.multiple_of(n * lanes, lanes), lanes)
            ng = (dot_nt(ab, wts[...]) * (1.0 / 256)).astype(BF).astype(F32)
            v = side_ref[s, :, at].astype(F32)
            n1, inv1 = norm_forward(v)
            nin = (n1 * tg).astype(BF)
            gate = dot_nn(gwt, nin)
            up = dot_nn(uwt, nin)
            sig = jax.nn.sigmoid(gate)
            act = gate * sig
            hidden = (act * up).astype(BF)
            n2, inv2 = norm_forward(v + dot_nn(dwt, hidden))
            mid = arrive_ref[s, :, at].astype(F32) + norm_backward(ng * og, n2, inv2)
            hg = dot_nn(dw, mid.astype(BF))
            gg = (hg * up * sig * (1.0 + gate * (1.0 - sig))).astype(BF)
            ug = (hg * act).astype(BF)
            nrg = dot_nn(gw, gg) + dot_nn(uw, ug)
            out_ref[s, :, at] = (mid + norm_backward(nrg * tg, n1, inv1)).astype(BF)

    for cp in store:
        cp.wait()


def tail(g, fin, side, arrive, lw, rw, og, tg, gw, uw, dw):
    hbm = pl.BlockSpec(memory_space=pl.ANY)
    return pl.pallas_call(
        tail_kernel,
        out_shape=(
            jax.ShapeDtypeStruct((64, 128, 128), BF),
            jax.ShapeDtypeStruct((2, 64, 1024), BF),
        ),
        in_specs=[hbm] + [VM] * 10,
        out_specs=(hbm, VM),
        scratch_shapes=[
            pltpu.VMEM((256, 256), BF),
            pltpu.VMEM((64, 128, 128), BF),
            pltpu.SemaphoreType.DMA((2, 4)),
        ],
        compiler_params=pltpu.CompilerParams(vmem_limit_bytes=67043328),
        name="tail",
    )(g, fin, side, arrive, lw, rw, og, tg, gw, uw, dw)


def per_device(
    pair_activation, target_distance_bins, distogram_weight, distogram_bias, outer_pair_weight,
    stored_lhs_operand, stored_rhs_operand, left_projection_weight, right_projection_weight,
    outer_mean_norm_gain, transition_norm_gain, gate_weight, up_weight, down_weight,
    side_stack_entry, arriving_stack_derivative,
):
    g, fin = main(
        pair_activation, target_distance_bins, distogram_weight.T, distogram_bias.reshape(1, -1),
        outer_pair_weight, stored_lhs_operand, stored_rhs_operand,
    )
    g, out = tail(
        g, fin, side_stack_entry, arriving_stack_derivative, left_projection_weight.T,
        right_projection_weight.T, outer_mean_norm_gain.reshape(1, -1),
        transition_norm_gain.reshape(1, -1), gate_weight, up_weight, down_weight.T,
    )
    return g, out


def solution(mesh):
    return jax.shard_map(
        per_device,
        mesh=mesh,
        in_specs=(
            P("row", "col", None),
            P("row", "col"),
            P(),
            P(),
            P(),
            P("row", None, "col"),
            P("row", None, "col"),
            P(),
            P(),
            P(),
            P(),
            P(),
            P(),
            P(),
            P(("row", "col"), None, None),
            P(("row", "col"), None, None),
        ),
        out_specs=(P("row", "col", None), P(("row", "col"), None, None)),
        check_vma=False,
    )
```

```python
import functools

import jax
import jax.numpy as jnp
from jax import lax
from jax.experimental import pallas as pl
from jax.experimental.pallas import tpu as pltpu
from jax.sharding import PartitionSpec as P

MESH = pl.DeviceIdType.MESH
BF = jnp.bfloat16
F32 = jnp.float32
VM = pl.BlockSpec(memory_space=pltpu.VMEM)


def dot_nt(a, b):
    return lax.dot_general(a, b, (((1,), (1,)), ((), ())), preferred_element_type=F32)


def dot_nn(a, b):
    return lax.dot_general(a, b, (((1,), (0,)), ((), ())), preferred_element_type=F32)


def place():
    row, col = lax.axis_index("row"), lax.axis_index("col")
    return row, col, row // 8, (row // 2) % 4, row % 2, col // 4, col % 4


def greet_all(row, col):
    barrier = pltpu.get_barrier_semaphore()
    me = row * 8 + col

    def greet(step, _):
        other = (me + step) % 128
        pl.semaphore_signal(
            barrier, inc=1, device_id={"row": other // 8, "col": other % 8}, device_id_type=MESH
        )
        return 0

    lax.fori_loop(1, 128, greet, 0)
    return barrier


def remote(src, dst, send, recv, row, col):
    return pltpu.make_async_remote_copy(
        src, dst, send, recv, device_id={"row": row, "col": col}, device_id_type=MESH
    )


def pair_index(pos):
    block, m = pos // 4, pos % 4
    return 2 * block + m % 2 + 16 * (m // 2)


def bias_columns(bias_ref):
    return jnp.broadcast_to(bias_ref[...], (128, 64)).T


def arrived(dst, recv, row, col):
    remote(dst, dst, recv, recv, row, col).wait_recv()


def norm_forward(v):
    centered = v - jnp.mean(v, axis=0, keepdims=True)
    inv = lax.rsqrt(jnp.mean(centered * centered, axis=0, keepdims=True) + 1e-05)
    return centered * inv, inv


def norm_backward(g, normed, inv):
    first = jnp.mean(g, axis=0, keepdims=True)
    second = jnp.mean(g * normed, axis=0, keepdims=True)
    return inv * (g - first - normed * second)


def column(ref):
    return jnp.broadcast_to(ref[...], (128, ref.shape[1])).T[:, :1]


UNITS = ((True, (0, 1)), (False, (2, 3)), (True, (4, 5)), (False, (6,)), (True, (7,)))
SCHEDULE = (
    (0, 0), (0, 1), (0, 2), (0, 3), (1, 0), (0, 4), (1, 1), (1, 2), (1, 3), (2, 0), (1, 4), (2, 1), (2, 2), (2, 3), (2, 4)
)


def main_kernel(
    a_hbm, tgt_ref, wd_ref, bias_ref, wo_ref, lhs_ref, rhs_ref, side_hbm, arrive_hbm, lw_ref, rw_ref, og_ref,
    tg_ref, gw_ref, uw_ref, dw_ref, g_hbm, out_ref, a_ref, side_ref, arrive_ref, fin_ref, n2_buf, inv_buf, wts, de_buf, a32, t_buf, b_buf, ra_buf, rb_buf, s32, lrg, g_buf, w32, wec, xs, o32, fin32, fin16, own_buf, gt_buf,
    *rest,
):
    n_units = len(UNITS)
    parts, gots_y, gots_z = rest[:n_units], rest[n_units : 2 * n_units], rest[2 * n_units : 3 * n_units]
    (
    de_send, de_recv, in_sem, loc_sem, m_send, m_recv, ra_send, ra_recv, rb_send, rb_recv,
    gx_send, gx_recv, p_send, p_recv, out_sem, y_send, y_recv, z_send, z_recv, f_send, f_recv,
    ) = rest[3 * n_units :]
    row, col, yh, x, k, yl, z = place()
    chip = row // 2
    diag = x == z
    same_y = yh == yl
    home = jnp.logical_and(diag, same_y)
    partner = row + 1 - 2 * k
    sends = []

    def go(cp, when=None):
        if when is None:
            cp.start()
        else:
            pl.when(when)(cp.start)
        sends.append((cp, when))

    def block_rows(r):
        return pl.ds(pl.multiple_of(r * 16, 16), 16)

    def x_row(r, d):
        return (r // 8) * 8 + (((r // 2) % 4 + d) % 4) * 2 + r % 2

    barrier = greet_all(row, col)
    loads = [
        pltpu.make_async_copy(a_hbm.at[pl.ds(n * 16, 16)], a_ref.at[pl.ds(n * 16, 16)], in_sem.at[n])
        for n in range(4)
    ]
    loads.append(pltpu.make_async_copy(side_hbm, side_ref, in_sem.at[4]))
    loads.append(pltpu.make_async_copy(arrive_hbm, arrive_ref, in_sem.at[5]))
    for cp in loads:
        cp.start()
    mine = block_rows(row)
    for side, ref in ((0, lhs_ref), (1, rhs_ref)):
        for s in range(16):
            s32[pl.ds(s * 32, 32), :] = ref[s].astype(F32)
        for e in range(32):
            lrg[side, mine, e * 128 : (e + 1) * 128] = s32[pl.ds(e, 16, stride=32), :].astype(BF)

    def whole(r):
        return lrg.at[:, block_rows(r)]

    def share(r, slot):
        go(remote(whole(r), whole(r), p_send.at[slot], p_recv.at[slot], partner, col))

    def gather_send(r, slot, there):
        go(pass_copy(r, slot, there))

    def pass_copy(r, slot, there):
        return remote(whole(r), whole(r), gx_send.at[slot], gx_recv.at[slot], there, col)

    def gather_wait(r, slot):
        arrived(whole(r), gx_recv.at[slot], row, col)

    flip = (row + 8) % 16
    left, right = x_row(row, 3), x_row(row, 1)
    flip_left, flip_right = x_row(flip, 3), x_row(flip, 1)
    far, flip_far = x_row(row, 2), x_row(flip, 2)
    wdt = wd_ref[...]
    wd = wdt.astype(F32).T.astype(BF)
    bias = bias_columns(bias_ref)

    for n in range(4):
        loads[n].wait()

        @pl.loop(0, 16, unroll=4)
        def _(p):
            i = n * 16 + p
            a32[pl.ds(pl.multiple_of(i * 128, 128), 128), :] = a_ref[i].astype(F32)

    for q in range(4):
        for kk in range(2):

            @pl.loop(0, 8, unroll=8)
            def _(p):
                ii = pair_index(q * 8 + p) + 64 * kk
                first = a32[pl.ds(ii + 32 * k, 64, stride=128), :]
                second = a32[pl.ds(ii + 32 * (1 - k), 64, stride=128), :]
                both = jnp.concatenate([first, second], axis=0).astype(BF)
                t_buf[kk, q, p] = (dot_nt(wdt, both) + bias).astype(BF)

            if q == 0 and kk == 0:
                pl.semaphore_wait(barrier, 127)
                gather_send(row, 0, flip)
                gather_send(row, 1, right)
                gather_send(row, 2, left)
                share(row, 0)
            src = t_buf.at[kk, q]
            final = remote(src, b_buf.at[k, q], m_send.at[kk, q], m_recv.at[k, q], 2 * col + kk, chip)
            local = pltpu.make_async_copy(src, b_buf.at[k, q], loc_sem.at[q])
            own = jnp.logical_and(home, k == kk)
            if q % 2 == 0:
                direct = jnp.logical_and(jnp.logical_or(diag, same_y), jnp.logical_not(own))
                if q == 0:
                    hop = remote(
                        src, ra_buf.at[kk, 0], m_send.at[kk, q], ra_recv.at[kk, 0],
                        yl * 8 + x * 2 + k, yh * 4 + z,
                    )
                else:
                    hop = remote(
                        src, de_buf.at[0, kk], m_send.at[kk, q], de_recv.at[0, kk],
                        yh * 8 + x * 2 + k, (1 - yl) * 4 + z,
                    )
            else:
                direct = jnp.logical_and(diag, jnp.logical_not(own))
                slot = (z - x + 3) % 4
                hop = remote(
                    src, rb_buf.at[slot, kk, q // 2], m_send.at[kk, q], rb_recv.at[slot, kk, q // 2],
                    yl * 8 + x * 2 + k, yh * 4 + x,
                )
            relayed = jnp.logical_not(jnp.logical_or(direct, own))
            pl.when(own)(local.start)
            pl.when(direct)(final.start)
            pl.when(relayed)(hop.start)
            sends.append((final, jnp.logical_not(own)))

    w32[...] = wo_ref[...].astype(F32)
    for e in range(32):
        wec[pl.ds(e * 32, 32), :] = w32[pl.ds(e, 32, stride=32), :].astype(BF)

    gather_wait(flip, 0)
    gather_send(flip, 3, right)
    gather_send(flip, 4, left)
    share(flip, 1)

    upward = z % 2 == 1

    def pass_on(near_left, near_right, slots, shares):
        gather_wait(near_left, slots[0])
        go(pass_copy(near_left, slots[2], right), upward)
        share(near_left, shares[0])
        gather_wait(near_right, slots[1])
        go(pass_copy(near_right, slots[2], left), jnp.logical_not(upward))
        share(near_right, shares[1])

    relay_a = jnp.logical_not(jnp.logical_or(diag, same_y))

    carrier = jnp.logical_and(same_y, jnp.logical_not(diag))

    def detour(leg):
        for kk in range(2):
            pl.when(carrier)(functools.partial(arrived, de_buf.at[leg, kk], de_recv.at[leg, kk], row, col))
            if leg == 0:
                dst, recv = de_buf.at[1, kk], de_recv.at[1, kk]
                there = ((1 - yh) * 8 + x * 2 + k, (1 - yl) * 4 + z)
            else:
                dst, recv = ra_buf.at[kk, 1], ra_recv.at[kk, 1]
                there = (yh * 8 + x * 2 + k, (1 - yl) * 4 + z)
            go(remote(de_buf.at[leg, kk], dst, de_send.at[leg, kk], recv, *there), carrier)

    def relay(j):
        for kk in range(2):
            pl.when(relay_a)(functools.partial(arrived, ra_buf.at[kk, j], ra_recv.at[kk, j], row, col))
            go(
                remote(
                    ra_buf.at[kk, j], b_buf.at[k, 2 * j], ra_send.at[kk, j], m_recv.at[k, 2 * j],
                    2 * (yh * 4 + z) + kk, yl * 4 + x,
                ),
                relay_a,
            )
        for kk in range(2):
            for slot in range(3):
                zs = (x + 1 + slot) % 4
                pl.when(diag)(
                    functools.partial(arrived, rb_buf.at[slot, kk, j], rb_recv.at[slot, kk, j], row, col)
                )
                go(
                    remote(
                        rb_buf.at[slot, kk, j], b_buf.at[k, 2 * j + 1], rb_send.at[slot, kk, j],
                        m_recv.at[k, 2 * j + 1], 2 * (yh * 4 + zs) + kk, yl * 4 + x,
                    ),
                    diag,
                )

    @pl.loop(0, 64, unroll=8)
    def _(i):
        own_buf[i] = (dot_nt(wdt, a_ref[i]) + bias).astype(BF)

    relay(0)
    pass_on(left, right, (1, 2, 5), (2, 3))
    detour(0)
    for cp in loads[4:]:
        cp.wait()
    gw, uw, dwt = gw_ref[...], uw_ref[...], dw_ref[...]
    gwt, uwt = gw.astype(F32).T.astype(BF), uw.astype(F32).T.astype(BF)
    og, tg = column(og_ref), column(tg_ref)

    def keep(s, n, which):
        base = ((s * 4 + n) * 2 + which) * 512
        return [pl.ds(pl.multiple_of(base + 256 * t, 256), 256) for t in range(2)]

    def transition(s):
        @pl.loop(0, 4)
        def _(n):
            at = pl.ds(pl.multiple_of(n * 256, 256), 256)
            v = side_ref[s, :, at].astype(F32)
            n1, _ = norm_forward(v)
            nin = (n1 * tg).astype(BF)
            gate, up = dot_nn(gwt, nin), dot_nn(uwt, nin)
            hidden = (gate * jax.nn.sigmoid(gate) * up).astype(BF)
            n2, inv2 = norm_forward(v + dot_nn(dwt, hidden))
            n2_buf[s, :, at] = n2
            inv_buf[s, :, at] = jnp.broadcast_to(inv2, (8, 256))
            for which, value in ((0, gate), (1, up)):
                for t, rows in enumerate(keep(s, n, which)):
                    a32[rows, :] = value[:, t * 128 : (t + 1) * 128]

    transition(0)
    detour(1)
    pass_on(flip_left, flip_right, (3, 4, 6), (4, 5))
    relay(1)
    transition(1)

    lane = lax.broadcasted_iota(jnp.int32, (64, 128), 1)
    level = lax.broadcasted_iota(jnp.int32, (64, 128), 0)
    low = lane < 64
    out_copies = []
    for q in range(4):
        for kk in range(2):
            own = jnp.logical_and(home, k == kk)
            pl.when(jnp.logical_not(own))(
                functools.partial(arrived, b_buf.at[kk, q], m_recv.at[kk, q], row, col)
            )
            pl.when(own)(pltpu.make_async_copy(t_buf.at[kk, q], b_buf.at[kk, q], loc_sem.at[q]).wait)

        @pl.loop(0, 8, unroll=4)
        def _(p):
            pos = q * 8 + p
            ii = pair_index(pos)
            b0 = b_buf[0, q, p].astype(F32)
            b1 = b_buf[1, q, p].astype(F32)
            mirrored = (
                jnp.where(low, b0, b1),
                pltpu.roll(jnp.where(low, b1, b0), 64, 1),
            )
            grads = []
            for h in range(2):
                i = ii + 32 * h
                sym = own_buf[i].astype(F32) + mirrored[h]
                top = jnp.max(sym, axis=0, keepdims=True)
                ex = jnp.exp(sym - top)
                prob = ex / jnp.sum(ex, axis=0, keepdims=True)
                tgt = tgt_ref[pl.ds(i, 1), :]
                hot = jnp.where(level == tgt, 1.0, 0.0)
                grad = 2.0 * (prob - hot)
                g_buf[i] = dot_nn(grad.T.astype(BF), wdt).astype(BF)
                grads.append(grad.astype(BF))
            gt_buf[p] = dot_nn(wd, jnp.concatenate(grads, axis=1)).astype(BF)

        @pl.loop(0, 8, unroll=2)
        def _(p):
            pos = q * 8 + p
            block, m = pos // 4, pos % 4
            gt = gt_buf[p]
            for side, w in ((0, wec), (1, wo_ref)):
                for n in range(4):
                    u = dot_nn(w[pl.ds(n * 256, 256), :], gt).astype(BF)
                    for h in range(2):
                        base = pl.multiple_of((m % 2) * 128 + (m // 2) * 32 + 64 * h, 32)
                        for f in range(8):
                            e = n * 8 + f
                            xs[side, block, pl.ds(base, 32), e * 128 : (e + 1) * 128] = u[
                                f * 32 : (f + 1) * 32, h * 128 : (h + 1) * 128
                            ]

        for lo in range(4):
            rows = pl.ds(lo * 16 + 4 * q, 4)
            cp = pltpu.make_async_copy(g_buf.at[rows], g_hbm.at[rows], out_sem.at[q, lo])
            cp.start()
            out_copies.append(cp)

    gather_wait(far, 5)
    share(far, 6)
    gather_wait(flip_far, 6)
    share(flip_far, 7)
    for slot, r in enumerate((row, flip, left, right, flip_left, flip_right, far, flip_far)):
        r = r + 1 - 2 * k
        arrived(whole(r), p_recv.at[slot], row, col)

    other = 1 - yl

    def contract(u):
        y_first, blocks = UNITS[u]
        part = parts[u]
        for n, block in enumerate(blocks):
            for side in range(2):
                out = dot_nt(lrg[1 - side], xs[side, block])
                for half in range(2):
                    o32[...] = out[:, half * 128 : (half + 1) * 128]
                    for w in range(16):
                        y2, z2 = w // 8, (w // 2) % 4
                        at = (y2, z2) if y_first else (z2, y2)
                        part[at[0], at[1], n, side, half, (w % 2) * 16 : (w % 2) * 16 + 16, :] = o32[
                            pl.ds(w, 16, stride=16), :
                        ].astype(BF)
        if y_first:
            go(remote(part.at[other], gots_y[u], y_send.at[u], y_recv.at[u], row, other * 4 + z))
        else:
            for d in range(1, 4):
                zz = (z + d) % 4
                go(remote(part.at[zz], gots_z[u].at[d - 1], z_send.at[u, d - 1], z_recv.at[u, d - 1], row, yl * 4 + zz))

    def tiles(u):
        return [(n, side, half) for n in range(len(UNITS[u][1])) for side in range(2) for half in range(2)]

    def second(u):
        part = parts[u]
        if UNITS[u][0]:
            arrived(gots_y[u], y_recv.at[u], row, col)
            for z2 in range(4):
                for at in tiles(u):
                    part[(yl, z2) + at] = (part[(yl, z2) + at].astype(F32) + gots_y[u][(z2,) + at].astype(F32)).astype(BF)
            for d in range(1, 4):
                zz = (z + d) % 4
                go(
                    remote(
                        part.at[yl, zz], gots_z[u].at[d - 1], z_send.at[u, d - 1], z_recv.at[u, d - 1],
                        row, yl * 4 + zz,
                    )
                )
        else:
            for d in range(1, 4):
                arrived(gots_z[u].at[d - 1], z_recv.at[u, d - 1], row, col)
            for y2 in range(2):
                for at in tiles(u):
                    total = part[(z, y2) + at].astype(F32)
                    for d in range(3):
                        total += gots_z[u][(d, y2) + at].astype(F32)
                    part[(z, y2) + at] = total.astype(BF)
            go(remote(part.at[z, other], gots_y[u], y_send.at[u], y_recv.at[u], row, other * 4 + z))

    def third(u):
        y_first, blocks = UNITS[u]
        if y_first:
            for d in range(1, 4):
                arrived(gots_z[u].at[d - 1], z_recv.at[u, d - 1], row, col)
        else:
            arrived(gots_y[u], y_recv.at[u], row, col)
        for at in tiles(u):
            if y_first:
                total = parts[u][(yl, z) + at].astype(F32)
                for d in range(3):
                    total += gots_z[u][(d,) + at].astype(F32)
            else:
                total = parts[u][(z, yl) + at].astype(F32) + gots_y[u][at].astype(F32)
            n, side, half = at
            tile = side * 16 + blocks[n] * 2 + half
            for t in range(2):
                fin32[pl.ds(t * 32 + tile, 16, stride=64), :] = total[t * 16 : (t + 1) * 16]

    for stage, u in SCHEDULE:
        (contract, second, third)[stage](u)

    for there in range(16):
        fin16[there] = fin32[pl.ds(there * 64, 64), :].astype(BF)
    fin_ref[row] = fin16[row]
    for step in range(1, 16):
        there = (row + step) % 16
        go(remote(fin16.at[there], fin_ref.at[row], f_send.at[step], f_recv.at[step], there, col))
    for step in range(1, 16):
        source = (row - step + 16) % 16
        arrived(fin_ref.at[source], f_recv.at[step], row, col)
    dw = dwt.astype(F32).T.astype(BF)
    ab = jnp.concatenate([lw_ref[...]] * 4 + [rw_ref[...]] * 4, axis=0).astype(F32).T.astype(BF)
    group = lax.broadcasted_iota(jnp.int32, (16, 128), 1) // 32
    zero = jnp.zeros((16, 128), BF)

    @pl.loop(0, 2)
    def _(s):
        @pl.loop(0, 4)
        def _(n):
            for r in range(4):
                for side in range(2):
                    rows = fin_ref[n * 4 + r, pl.ds(pl.multiple_of(s * 32 + side * 16, 16), 16), :]
                    for lo in range(4):
                        wts[pl.ds(r * 64 + lo * 16, 16), side * 128 : side * 128 + 128] = jnp.where(
                            group == lo, rows, zero
                        )
            at = pl.ds(pl.multiple_of(n * 256, 256), 256)
            ng = (dot_nt(ab, wts[...]) * (1.0 / 256)).astype(BF).astype(F32)
            mid = arrive_ref[s, :, at].astype(F32) + norm_backward(ng * og, n2_buf[s, :, at], inv_buf[s, :1, at])
            hg = dot_nn(dw, mid.astype(BF))
            gate, up = [
                jnp.concatenate([a32[rows, :] for rows in keep(s, n, which)], axis=1) for which in range(2)
            ]
            sig = jax.nn.sigmoid(gate)
            act = gate * sig
            gg = (hg * up * sig * (1.0 + gate * (1.0 - sig))).astype(BF)
            ug = (hg * act).astype(BF)
            nrg = dot_nn(gw, gg) + dot_nn(uw, ug)
            n1, inv1 = norm_forward(side_ref[s, :, at].astype(F32))
            out_ref[s, :, at] = (mid + norm_backward(nrg * tg, n1, inv1)).astype(BF)

    for cp, when in sends:
        if when is None:
            cp.wait_send()
        else:
            pl.when(when)(cp.wait_send)
    for cp in out_copies:
        cp.wait()


def main(*args):
    dma = pltpu.SemaphoreType.DMA
    hbm = pl.BlockSpec(memory_space=pl.ANY)
    return pl.pallas_call(
        main_kernel,
        out_shape=(
            jax.ShapeDtypeStruct((64, 128, 128), BF),
            jax.ShapeDtypeStruct((2, 64, 1024), BF),
        ),
        in_specs=[hbm] + [VM] * 6 + [hbm, hbm] + [VM] * 7,
        out_specs=(hbm, VM),
        scratch_shapes=[
            pltpu.VMEM((64, 128, 128), BF),
            pltpu.VMEM((2, 64, 1024), BF),
            pltpu.VMEM((2, 64, 1024), BF),
            pltpu.VMEM((16, 64, 128), BF),
            pltpu.VMEM((2, 64, 1024), F32),
            pltpu.VMEM((2, 8, 1024), F32),
            pltpu.VMEM((256, 256), BF),
            pltpu.VMEM((2, 2, 8, 64, 128), BF),
            pltpu.VMEM((8192, 128), F32),
            pltpu.VMEM((2, 4, 8, 64, 128), BF),
            pltpu.VMEM((2, 4, 8, 64, 128), BF),
            pltpu.VMEM((2, 2, 8, 64, 128), BF),
            pltpu.VMEM((3, 2, 2, 8, 64, 128), BF),
            pltpu.VMEM((512, 128), F32),
            pltpu.VMEM((2, 256, 4096), BF),
            pltpu.VMEM((64, 128, 128), BF),
            pltpu.VMEM((1024, 128), F32),
            pltpu.VMEM((1024, 128), BF),
            pltpu.VMEM((2, 8, 256, 4096), BF),
            pltpu.VMEM((256, 128), F32),
            pltpu.VMEM((1024, 128), F32),
            pltpu.VMEM((16, 64, 128), BF),
            pltpu.VMEM((64, 64, 128), BF),
            pltpu.VMEM((8, 128, 256), BF),
            *[pltpu.VMEM(((2, 4) if y else (4, 2)) + (len(b), 2, 2, 32, 128), BF) for y, b in UNITS],
            *[pltpu.VMEM(((4,) if y else ()) + (len(b), 2, 2, 32, 128), BF) for y, b in UNITS],
            *[pltpu.VMEM(((3,) if y else (3, 2)) + (len(b), 2, 2, 32, 128), BF) for y, b in UNITS],
            dma((2, 2)),
            dma((2, 2)),
            dma((6,)),
            dma((4,)),
            dma((2, 4)),
            dma((2, 4)),
            dma((2, 2)),
            dma((2, 2)),
            dma((3, 2, 2)),
            dma((3, 2, 2)),
            dma((9,)),
            dma((9,)),
            dma((8,)),
            dma((8,)),
            dma((4, 4)),
            dma((8,)),
            dma((8,)),
            dma((8, 3)),
            dma((8, 3)),
            dma((16,)),
            dma((16,)),
        ],
        compiler_params=pltpu.CompilerParams(
            collective_id=0, has_side_effects=True, vmem_limit_bytes=67043328
        ),
        name="main",
    )(*args)


def hand_on_kernel(g_in, o_in, g_out, o_out, g_stage, o_stage, sem):
    pairs = [(g_in.at[pl.ds(n * 8, 8)], g_stage.at[pl.ds(n * 8, 8)], g_out.at[pl.ds(n * 8, 8)]) for n in range(8)]
    pairs.append((o_in, o_stage, o_out))
    fetch = [pltpu.make_async_copy(a, b, sem.at[0, n]) for n, (a, b, _) in enumerate(pairs)]
    store = [pltpu.make_async_copy(b, c, sem.at[1, n]) for n, (_, b, c) in enumerate(pairs)]
    for cp in fetch:
        cp.start()
    for cp, back in zip(fetch, store):
        cp.wait()
        back.start()
    for back in store:
        back.wait()


def hand_on(g, out):
    hbm = pl.BlockSpec(memory_space=pl.ANY)
    return pl.pallas_call(
        hand_on_kernel,
        out_shape=(jax.ShapeDtypeStruct(g.shape, g.dtype), jax.ShapeDtypeStruct(out.shape, out.dtype)),
        in_specs=[hbm, hbm],
        out_specs=(hbm, hbm),
        scratch_shapes=[pltpu.VMEM(g.shape, BF), pltpu.VMEM(out.shape, BF), pltpu.SemaphoreType.DMA((2, 9))],
        compiler_params=pltpu.CompilerParams(vmem_limit_bytes=67043328),
        name="hand_on",
    )(g, out)


def per_device(
    pair_activation, target_distance_bins, distogram_weight, distogram_bias, outer_pair_weight,
    stored_lhs_operand, stored_rhs_operand, left_projection_weight, right_projection_weight,
    outer_mean_norm_gain, transition_norm_gain, gate_weight, up_weight, down_weight,
    side_stack_entry, arriving_stack_derivative,
):
    g, out = main(
        pair_activation, target_distance_bins, distogram_weight.T, distogram_bias.reshape(1, -1),
        outer_pair_weight, stored_lhs_operand, stored_rhs_operand, side_stack_entry,
        arriving_stack_derivative, left_projection_weight.T, right_projection_weight.T,
        outer_mean_norm_gain.reshape(1, -1), transition_norm_gain.reshape(1, -1), gate_weight, up_weight,
        down_weight.T,
    )
    return hand_on(g, out)


def solution(mesh):
    return jax.shard_map(
        per_device,
        mesh=mesh,
        in_specs=(
            P("row", "col", None),
            P("row", "col"),
            P(),
            P(),
            P(),
            P("row", None, "col"),
            P("row", None, "col"),
            P(),
            P(),
            P(),
            P(),
            P(),
            P(),
            P(),
            P(("row", "col"), None, None),
            P(("row", "col"), None, None),
        ),
        out_specs=(P("row", "col", None), P(("row", "col"), None, None)),
        check_vma=False,
    )
```

```python
import functools

import jax
import jax.numpy as jnp
from jax import lax
from jax.experimental import pallas as pl
from jax.experimental.pallas import tpu as pltpu
from jax.sharding import PartitionSpec as P

MESH = pl.DeviceIdType.MESH
BF = jnp.bfloat16
F32 = jnp.float32
VM = pl.BlockSpec(memory_space=pltpu.VMEM)


def dot_nt(a, b):
    return lax.dot_general(a, b, (((1,), (1,)), ((), ())), preferred_element_type=F32)


def dot_nn(a, b):
    return lax.dot_general(a, b, (((1,), (0,)), ((), ())), preferred_element_type=F32)


def place():
    row, col = lax.axis_index("row"), lax.axis_index("col")
    return row, col, row // 8, (row // 2) % 4, row % 2, col // 4, col % 4


def greet_all(row, col):
    barrier = pltpu.get_barrier_semaphore()
    me = row * 8 + col

    def greet(step, _):
        other = (me + step) % 128
        pl.semaphore_signal(
            barrier, inc=1, device_id={"row": other // 8, "col": other % 8}, device_id_type=MESH
        )
        return 0

    lax.fori_loop(1, 128, greet, 0)
    return barrier


def remote(src, dst, send, recv, row, col):
    return pltpu.make_async_remote_copy(
        src, dst, send, recv, device_id={"row": row, "col": col}, device_id_type=MESH
    )


def pair_index(pos):
    block, m = pos // 4, pos % 4
    return 2 * block + m % 2 + 16 * (m // 2)


def bias_columns(bias_ref):
    return jnp.broadcast_to(bias_ref[...], (128, 64)).T


def arrived(dst, recv, row, col):
    remote(dst, dst, recv, recv, row, col).wait_recv()


def norm_forward(v):
    centered = v - jnp.mean(v, axis=0, keepdims=True)
    inv = lax.rsqrt(jnp.mean(centered * centered, axis=0, keepdims=True) + 1e-05)
    return centered * inv, inv


def norm_backward(g, normed, inv):
    first = jnp.mean(g, axis=0, keepdims=True)
    second = jnp.mean(g * normed, axis=0, keepdims=True)
    return inv * (g - first - normed * second)


def column(ref):
    return jnp.broadcast_to(ref[...], (128, ref.shape[1])).T[:, :1]


UNITS = ((True, (0, 1)), (False, (2, 3)), (True, (4, 5)), (False, (6,)), (True, (7,)))
SCHEDULE = (
    (0, 0), (0, 1), (0, 2), (0, 3), (1, 0), (0, 4), (1, 1), (1, 2), (1, 3), (2, 0), (1, 4), (2, 1), (2, 2), (2, 3), (2, 4)
)


def main_kernel(
    a_hbm, tgt_ref, wd_ref, bias_ref, wo_ref, lhs_ref, rhs_ref, side_hbm, arrive_hbm, lw_ref, rw_ref, og_ref,
    tg_ref, gw_ref, uw_ref, dw_ref, g_hbm, out_ref, a_ref, side_ref, arrive_ref, fin_ref, n2_buf, inv_buf, wts, de_buf, a32, t_buf, b_buf, ra_buf, rb_buf, s32, lrg, g_buf, w32, wec, xs, o32, fin32, fin16, own_buf, gt_buf,
    *rest,
):
    n_units = len(UNITS)
    parts, gots_y, gots_z = rest[:n_units], rest[n_units : 2 * n_units], rest[2 * n_units : 3 * n_units]
    (
    de_send, de_recv, in_sem, loc_sem, m_send, m_recv, ra_send, ra_recv, rb_send, rb_recv,
    gx_send, gx_recv, p_send, p_recv, out_sem, y_send, y_recv, z_send, z_recv, f_send, f_recv,
    ) = rest[3 * n_units :]
    row, col, yh, x, k, yl, z = place()
    chip = row // 2
    diag = x == z
    same_y = yh == yl
    home = jnp.logical_and(diag, same_y)
    partner = row + 1 - 2 * k
    sends = []

    def go(cp, when=None):
        if when is None:
            cp.start()
        else:
            pl.when(when)(cp.start)
        sends.append((cp, when))

    def block_rows(r):
        return pl.ds(pl.multiple_of(r * 16, 16), 16)

    def x_row(r, d):
        return (r // 8) * 8 + (((r // 2) % 4 + d) % 4) * 2 + r % 2

    barrier = greet_all(row, col)
    loads = [
        pltpu.make_async_copy(a_hbm.at[pl.ds(n * 16, 16)], a_ref.at[pl.ds(n * 16, 16)], in_sem.at[n])
        for n in range(4)
    ]
    loads.append(pltpu.make_async_copy(side_hbm, side_ref, in_sem.at[4]))
    loads.append(pltpu.make_async_copy(arrive_hbm, arrive_ref, in_sem.at[5]))
    for cp in loads:
        cp.start()
    mine = block_rows(row)
    for side, ref in ((0, lhs_ref), (1, rhs_ref)):
        for s in range(16):
            s32[pl.ds(s * 32, 32), :] = ref[s].astype(F32)
        for e in range(32):
            lrg[side, mine, e * 128 : (e + 1) * 128] = s32[pl.ds(e, 16, stride=32), :].astype(BF)

    def whole(r):
        return lrg.at[:, block_rows(r)]

    def share(r, slot):
        go(remote(whole(r), whole(r), p_send.at[slot], p_recv.at[slot], partner, col))

    def gather_send(r, slot, there):
        go(pass_copy(r, slot, there))

    def pass_copy(r, slot, there):
        return remote(whole(r), whole(r), gx_send.at[slot], gx_recv.at[slot], there, col)

    def gather_wait(r, slot):
        arrived(whole(r), gx_recv.at[slot], row, col)

    flip = (row + 8) % 16
    left, right = x_row(row, 3), x_row(row, 1)
    flip_left, flip_right = x_row(flip, 3), x_row(flip, 1)
    far, flip_far = x_row(row, 2), x_row(flip, 2)
    wdt = wd_ref[...]
    wd = wdt.astype(F32).T.astype(BF)
    bias = bias_columns(bias_ref)

    for n in range(4):
        loads[n].wait()

        @pl.loop(0, 16, unroll=4)
        def _(p):
            i = n * 16 + p
            a32[pl.ds(pl.multiple_of(i * 128, 128), 128), :] = a_ref[i].astype(F32)

    for q in range(4):
        for kk in range(2):

            @pl.loop(0, 8, unroll=8)
            def _(p):
                ii = pair_index(q * 8 + p) + 64 * kk
                first = a32[pl.ds(ii + 32 * k, 64, stride=128), :]
                second = a32[pl.ds(ii + 32 * (1 - k), 64, stride=128), :]
                both = jnp.concatenate([first, second], axis=0).astype(BF)
                t_buf[kk, q, p] = (dot_nt(wdt, both) + bias).astype(BF)

            if q == 0 and kk == 0:
                pl.semaphore_wait(barrier, 127)
                gather_send(row, 0, flip)
                gather_send(row, 1, right)
                gather_send(row, 2, left)
                share(row, 0)
            src = t_buf.at[kk, q]
            final = remote(src, b_buf.at[k, q], m_send.at[kk, q], m_recv.at[k, q], 2 * col + kk, chip)
            local = pltpu.make_async_copy(src, b_buf.at[k, q], loc_sem.at[q])
            own = jnp.logical_and(home, k == kk)
            if q % 2 == 0:
                direct = jnp.logical_and(jnp.logical_or(diag, same_y), jnp.logical_not(own))
                if q == 0:
                    hop = remote(
                        src, ra_buf.at[kk, 0], m_send.at[kk, q], ra_recv.at[kk, 0],
                        yl * 8 + x * 2 + k, yh * 4 + z,
                    )
                else:
                    hop = remote(
                        src, de_buf.at[0, kk], m_send.at[kk, q], de_recv.at[0, kk],
                        yh * 8 + x * 2 + k, (1 - yl) * 4 + z,
                    )
            else:
                direct = jnp.logical_and(diag, jnp.logical_not(own))
                slot = (z - x + 3) % 4
                hop = remote(
                    src, rb_buf.at[slot, kk, q // 2], m_send.at[kk, q], rb_recv.at[slot, kk, q // 2],
                    yl * 8 + x * 2 + k, yh * 4 + x,
                )
            relayed = jnp.logical_not(jnp.logical_or(direct, own))
            pl.when(own)(local.start)
            pl.when(direct)(final.start)
            pl.when(relayed)(hop.start)
            sends.append((final, jnp.logical_not(own)))

    w32[...] = wo_ref[...].astype(F32)
    for e in range(32):
        wec[pl.ds(e * 32, 32), :] = w32[pl.ds(e, 32, stride=32), :].astype(BF)

    gather_wait(flip, 0)
    gather_send(flip, 3, right)
    gather_send(flip, 4, left)
    share(flip, 1)

    upward = z % 2 == 1

    def pass_on(near_left, near_right, slots, shares):
        gather_wait(near_left, slots[0])
        go(pass_copy(near_left, slots[2], right), upward)
        share(near_left, shares[0])
        gather_wait(near_right, slots[1])
        go(pass_copy(near_right, slots[2], left), jnp.logical_not(upward))
        share(near_right, shares[1])

    relay_a = jnp.logical_not(jnp.logical_or(diag, same_y))

    carrier = jnp.logical_and(same_y, jnp.logical_not(diag))

    def detour(leg):
        for kk in range(2):
            pl.when(carrier)(functools.partial(arrived, de_buf.at[leg, kk], de_recv.at[leg, kk], row, col))
            if leg == 0:
                dst, recv = de_buf.at[1, kk], de_recv.at[1, kk]
                there = ((1 - yh) * 8 + x * 2 + k, (1 - yl) * 4 + z)
            else:
                dst, recv = ra_buf.at[kk, 1], ra_recv.at[kk, 1]
                there = (yh * 8 + x * 2 + k, (1 - yl) * 4 + z)
            go(remote(de_buf.at[leg, kk], dst, de_send.at[leg, kk], recv, *there), carrier)

    def relay(j):
        for kk in range(2):
            pl.when(relay_a)(functools.partial(arrived, ra_buf.at[kk, j], ra_recv.at[kk, j], row, col))
            go(
                remote(
                    ra_buf.at[kk, j], b_buf.at[k, 2 * j], ra_send.at[kk, j], m_recv.at[k, 2 * j],
                    2 * (yh * 4 + z) + kk, yl * 4 + x,
                ),
                relay_a,
            )
        for kk in range(2):
            for slot in range(3):
                zs = (x + 1 + slot) % 4
                pl.when(diag)(
                    functools.partial(arrived, rb_buf.at[slot, kk, j], rb_recv.at[slot, kk, j], row, col)
                )
                go(
                    remote(
                        rb_buf.at[slot, kk, j], b_buf.at[k, 2 * j + 1], rb_send.at[slot, kk, j],
                        m_recv.at[k, 2 * j + 1], 2 * (yh * 4 + zs) + kk, yl * 4 + x,
                    ),
                    diag,
                )

    @pl.loop(0, 64, unroll=8)
    def _(i):
        own_buf[i] = (dot_nt(wdt, a_ref[i]) + bias).astype(BF)

    relay(0)
    pass_on(left, right, (1, 2, 5), (2, 3))
    detour(0)
    for cp in loads[4:]:
        cp.wait()
    gw, uw, dwt = gw_ref[...], uw_ref[...], dw_ref[...]
    gwt, uwt = gw.astype(F32).T.astype(BF), uw.astype(F32).T.astype(BF)
    og, tg = column(og_ref), column(tg_ref)

    def keep(s, n, which):
        base = ((s * 4 + n) * 2 + which) * 512
        return [pl.ds(pl.multiple_of(base + 256 * t, 256), 256) for t in range(2)]

    def transition(s):
        @pl.loop(0, 4)
        def _(n):
            at = pl.ds(pl.multiple_of(n * 256, 256), 256)
            v = side_ref[s, :, at].astype(F32)
            n1, _ = norm_forward(v)
            nin = (n1 * tg).astype(BF)
            gate, up = dot_nn(gwt, nin), dot_nn(uwt, nin)
            hidden = (gate * jax.nn.sigmoid(gate) * up).astype(BF)
            n2, inv2 = norm_forward(v + dot_nn(dwt, hidden))
            n2_buf[s, :, at] = n2
            inv_buf[s, :, at] = jnp.broadcast_to(inv2, (8, 256))
            for which, value in ((0, gate), (1, up)):
                for t, rows in enumerate(keep(s, n, which)):
                    a32[rows, :] = value[:, t * 128 : (t + 1) * 128]

    transition(0)
    detour(1)
    relay(1)
    transition(1)

    lane = lax.broadcasted_iota(jnp.int32, (64, 128), 1)
    level = lax.broadcasted_iota(jnp.int32, (64, 128), 0)
    low = lane < 64
    out_copies = []
    for q in range(4):
        for kk in range(2):
            own = jnp.logical_and(home, k == kk)
            pl.when(jnp.logical_not(own))(
                functools.partial(arrived, b_buf.at[kk, q], m_recv.at[kk, q], row, col)
            )
            pl.when(own)(pltpu.make_async_copy(t_buf.at[kk, q], b_buf.at[kk, q], loc_sem.at[q]).wait)

        @pl.loop(0, 8, unroll=4)
        def _(p):
            pos = q * 8 + p
            ii = pair_index(pos)
            b0 = b_buf[0, q, p].astype(F32)
            b1 = b_buf[1, q, p].astype(F32)
            mirrored = (
                jnp.where(low, b0, b1),
                pltpu.roll(jnp.where(low, b1, b0), 64, 1),
            )
            grads = []
            for h in range(2):
                i = ii + 32 * h
                sym = own_buf[i].astype(F32) + mirrored[h]
                top = jnp.max(sym, axis=0, keepdims=True)
                ex = jnp.exp(sym - top)
                prob = ex / jnp.sum(ex, axis=0, keepdims=True)
                tgt = tgt_ref[pl.ds(i, 1), :]
                hot = jnp.where(level == tgt, 1.0, 0.0)
                grad = 2.0 * (prob - hot)
                g_buf[i] = dot_nn(grad.T.astype(BF), wdt).astype(BF)
                grads.append(grad.astype(BF))
            gt_buf[p] = dot_nn(wd, jnp.concatenate(grads, axis=1)).astype(BF)

        @pl.loop(0, 8, unroll=2)
        def _(p):
            pos = q * 8 + p
            block, m = pos // 4, pos % 4
            gt = gt_buf[p]
            for side, w in ((0, wec), (1, wo_ref)):
                for n in range(4):
                    u = dot_nn(w[pl.ds(n * 256, 256), :], gt).astype(BF)
                    for h in range(2):
                        base = pl.multiple_of((m % 2) * 128 + (m // 2) * 32 + 64 * h, 32)
                        for f in range(8):
                            e = n * 8 + f
                            xs[side, block, pl.ds(base, 32), e * 128 : (e + 1) * 128] = u[
                                f * 32 : (f + 1) * 32, h * 128 : (h + 1) * 128
                            ]

        for lo in range(4):
            rows = pl.ds(lo * 16 + 4 * q, 4)
            cp = pltpu.make_async_copy(g_buf.at[rows], g_hbm.at[rows], out_sem.at[q, lo])
            cp.start()
            out_copies.append(cp)
        if q == 0:
            pass_on(flip_left, flip_right, (3, 4, 6), (4, 5))

    gather_wait(far, 5)
    share(far, 6)
    gather_wait(flip_far, 6)
    share(flip_far, 7)
    for slot, r in enumerate((row, flip, left, right, flip_left, flip_right, far, flip_far)):
        r = r + 1 - 2 * k
        arrived(whole(r), p_recv.at[slot], row, col)

    other = 1 - yl

    def contract(u):
        y_first, blocks = UNITS[u]
        part = parts[u]
        for n, block in enumerate(blocks):
            for side in range(2):
                out = dot_nt(lrg[1 - side], xs[side, block])
                for half in range(2):
                    o32[...] = out[:, half * 128 : (half + 1) * 128]
                    for w in range(16):
                        y2, z2 = w // 8, (w // 2) % 4
                        at = (y2, z2) if y_first else (z2, y2)
                        part[at[0], at[1], n, side, half, (w % 2) * 16 : (w % 2) * 16 + 16, :] = o32[
                            pl.ds(w, 16, stride=16), :
                        ].astype(BF)
        if y_first:
            go(remote(part.at[other], gots_y[u], y_send.at[u], y_recv.at[u], row, other * 4 + z))
        else:
            for d in range(1, 4):
                zz = (z + d) % 4
                go(remote(part.at[zz], gots_z[u].at[d - 1], z_send.at[u, d - 1], z_recv.at[u, d - 1], row, yl * 4 + zz))

    def tiles(u):
        return [(n, side, half) for n in range(len(UNITS[u][1])) for side in range(2) for half in range(2)]

    def second(u):
        part = parts[u]
        if UNITS[u][0]:
            arrived(gots_y[u], y_recv.at[u], row, col)
            for z2 in range(4):
                for at in tiles(u):
                    part[(yl, z2) + at] = (part[(yl, z2) + at].astype(F32) + gots_y[u][(z2,) + at].astype(F32)).astype(BF)
            for d in range(1, 4):
                zz = (z + d) % 4
                go(
                    remote(
                        part.at[yl, zz], gots_z[u].at[d - 1], z_send.at[u, d - 1], z_recv.at[u, d - 1],
                        row, yl * 4 + zz,
                    )
                )
        else:
            for d in range(1, 4):
                arrived(gots_z[u].at[d - 1], z_recv.at[u, d - 1], row, col)
            for y2 in range(2):
                for at in tiles(u):
                    total = part[(z, y2) + at].astype(F32)
                    for d in range(3):
                        total += gots_z[u][(d, y2) + at].astype(F32)
                    part[(z, y2) + at] = total.astype(BF)
            go(remote(part.at[z, other], gots_y[u], y_send.at[u], y_recv.at[u], row, other * 4 + z))

    def third(u):
        y_first, blocks = UNITS[u]
        if y_first:
            for d in range(1, 4):
                arrived(gots_z[u].at[d - 1], z_recv.at[u, d - 1], row, col)
        else:
            arrived(gots_y[u], y_recv.at[u], row, col)
        for at in tiles(u):
            if y_first:
                total = parts[u][(yl, z) + at].astype(F32)
                for d in range(3):
                    total += gots_z[u][(d,) + at].astype(F32)
            else:
                total = parts[u][(z, yl) + at].astype(F32) + gots_y[u][at].astype(F32)
            n, side, half = at
            tile = side * 16 + blocks[n] * 2 + half
            for t in range(2):
                fin32[pl.ds(t * 32 + tile, 16, stride=64), :] = total[t * 16 : (t + 1) * 16]

    for stage, u in SCHEDULE:
        (contract, second, third)[stage](u)

    for there in range(16):
        fin16[there] = fin32[pl.ds(there * 64, 64), :].astype(BF)
    fin_ref[row] = fin16[row]
    for step in range(1, 16):
        there = (row + step) % 16
        go(remote(fin16.at[there], fin_ref.at[row], f_send.at[step], f_recv.at[step], there, col))
    for step in range(1, 16):
        source = (row - step + 16) % 16
        arrived(fin_ref.at[source], f_recv.at[step], row, col)
    dw = dwt.astype(F32).T.astype(BF)
    ab = jnp.concatenate([lw_ref[...]] * 4 + [rw_ref[...]] * 4, axis=0).astype(F32).T.astype(BF)
    group = lax.broadcasted_iota(jnp.int32, (16, 128), 1) // 32
    zero = jnp.zeros((16, 128), BF)

    @pl.loop(0, 2)
    def _(s):
        @pl.loop(0, 4, unroll=4)
        def _(n):
            for r in range(4):
                for side in range(2):
                    rows = fin_ref[n * 4 + r, pl.ds(pl.multiple_of(s * 32 + side * 16, 16), 16), :]
                    for lo in range(4):
                        wts[n, pl.ds(r * 64 + lo * 16, 16), side * 128 : side * 128 + 128] = jnp.where(
                            group == lo, rows, zero
                        )
            at = pl.ds(pl.multiple_of(n * 256, 256), 256)
            ng = (dot_nt(ab, wts[n]) * (1.0 / 256)).astype(BF).astype(F32)
            mid = arrive_ref[s, :, at].astype(F32) + norm_backward(ng * og, n2_buf[s, :, at], inv_buf[s, :1, at])
            hg = dot_nn(dw, mid.astype(BF))
            gate, up = [
                jnp.concatenate([a32[rows, :] for rows in keep(s, n, which)], axis=1) for which in range(2)
            ]
            sig = jax.nn.sigmoid(gate)
            act = gate * sig
            gg = (hg * up * sig * (1.0 + gate * (1.0 - sig))).astype(BF)
            ug = (hg * act).astype(BF)
            nrg = dot_nn(gw, gg) + dot_nn(uw, ug)
            n1, inv1 = norm_forward(side_ref[s, :, at].astype(F32))
            out_ref[s, :, at] = (mid + norm_backward(nrg * tg, n1, inv1)).astype(BF)

    for cp, when in sends:
        if when is None:
            cp.wait_send()
        else:
            pl.when(when)(cp.wait_send)
    for cp in out_copies:
        cp.wait()


def main(*args):
    dma = pltpu.SemaphoreType.DMA
    hbm = pl.BlockSpec(memory_space=pl.ANY)
    return pl.pallas_call(
        main_kernel,
        out_shape=(
            jax.ShapeDtypeStruct((64, 128, 128), BF),
            jax.ShapeDtypeStruct((2, 64, 1024), BF),
        ),
        in_specs=[hbm] + [VM] * 6 + [hbm, hbm] + [VM] * 7,
        out_specs=(hbm, VM),
        scratch_shapes=[
            pltpu.VMEM((64, 128, 128), BF),
            pltpu.VMEM((2, 64, 1024), BF),
            pltpu.VMEM((2, 64, 1024), BF),
            pltpu.VMEM((16, 64, 128), BF),
            pltpu.VMEM((2, 64, 1024), F32),
            pltpu.VMEM((2, 8, 1024), F32),
            pltpu.VMEM((4, 256, 256), BF),
            pltpu.VMEM((2, 2, 8, 64, 128), BF),
            pltpu.VMEM((8192, 128), F32),
            pltpu.VMEM((2, 4, 8, 64, 128), BF),
            pltpu.VMEM((2, 4, 8, 64, 128), BF),
            pltpu.VMEM((2, 2, 8, 64, 128), BF),
            pltpu.VMEM((3, 2, 2, 8, 64, 128), BF),
            pltpu.VMEM((512, 128), F32),
            pltpu.VMEM((2, 256, 4096), BF),
            pltpu.VMEM((64, 128, 128), BF),
            pltpu.VMEM((1024, 128), F32),
            pltpu.VMEM((1024, 128), BF),
            pltpu.VMEM((2, 8, 256, 4096), BF),
            pltpu.VMEM((256, 128), F32),
            pltpu.VMEM((1024, 128), F32),
            pltpu.VMEM((16, 64, 128), BF),
            pltpu.VMEM((64, 64, 128), BF),
            pltpu.VMEM((8, 128, 256), BF),
            *[pltpu.VMEM(((2, 4) if y else (4, 2)) + (len(b), 2, 2, 32, 128), BF) for y, b in UNITS],
            *[pltpu.VMEM(((4,) if y else ()) + (len(b), 2, 2, 32, 128), BF) for y, b in UNITS],
            *[pltpu.VMEM(((3,) if y else (3, 2)) + (len(b), 2, 2, 32, 128), BF) for y, b in UNITS],
            dma((2, 2)),
            dma((2, 2)),
            dma((6,)),
            dma((4,)),
            dma((2, 4)),
            dma((2, 4)),
            dma((2, 2)),
            dma((2, 2)),
            dma((3, 2, 2)),
            dma((3, 2, 2)),
            dma((9,)),
            dma((9,)),
            dma((8,)),
            dma((8,)),
            dma((4, 4)),
            dma((8,)),
            dma((8,)),
            dma((8, 3)),
            dma((8, 3)),
            dma((16,)),
            dma((16,)),
        ],
        compiler_params=pltpu.CompilerParams(
            collective_id=0, has_side_effects=True, vmem_limit_bytes=67043328
        ),
        name="main",
    )(*args)


def hand_on_kernel(g_in, o_in, g_out, o_out, g_stage, o_stage, sem):
    pairs = [(g_in.at[pl.ds(n * 8, 8)], g_stage.at[pl.ds(n * 8, 8)], g_out.at[pl.ds(n * 8, 8)]) for n in range(8)]
    pairs.append((o_in, o_stage, o_out))
    fetch = [pltpu.make_async_copy(a, b, sem.at[0, n]) for n, (a, b, _) in enumerate(pairs)]
    store = [pltpu.make_async_copy(b, c, sem.at[1, n]) for n, (_, b, c) in enumerate(pairs)]
    for cp in fetch:
        cp.start()
    for cp, back in zip(fetch, store):
        cp.wait()
        back.start()
    for back in store:
        back.wait()


def hand_on(g, out):
    hbm = pl.BlockSpec(memory_space=pl.ANY)
    return pl.pallas_call(
        hand_on_kernel,
        out_shape=(jax.ShapeDtypeStruct(g.shape, g.dtype), jax.ShapeDtypeStruct(out.shape, out.dtype)),
        in_specs=[hbm, hbm],
        out_specs=(hbm, hbm),
        scratch_shapes=[pltpu.VMEM(g.shape, BF), pltpu.VMEM(out.shape, BF), pltpu.SemaphoreType.DMA((2, 9))],
        compiler_params=pltpu.CompilerParams(vmem_limit_bytes=67043328),
        name="hand_on",
    )(g, out)


def per_device(
    pair_activation, target_distance_bins, distogram_weight, distogram_bias, outer_pair_weight,
    stored_lhs_operand, stored_rhs_operand, left_projection_weight, right_projection_weight,
    outer_mean_norm_gain, transition_norm_gain, gate_weight, up_weight, down_weight,
    side_stack_entry, arriving_stack_derivative,
):
    g, out = main(
        pair_activation, target_distance_bins, distogram_weight.T, distogram_bias.reshape(1, -1),
        outer_pair_weight, stored_lhs_operand, stored_rhs_operand, side_stack_entry,
        arriving_stack_derivative, left_projection_weight.T, right_projection_weight.T,
        outer_mean_norm_gain.reshape(1, -1), transition_norm_gain.reshape(1, -1), gate_weight, up_weight,
        down_weight.T,
    )
    return hand_on(g, out)


def solution(mesh):
    return jax.shard_map(
        per_device,
        mesh=mesh,
        in_specs=(
            P("row", "col", None),
            P("row", "col"),
            P(),
            P(),
            P(),
            P("row", None, "col"),
            P("row", None, "col"),
            P(),
            P(),
            P(),
            P(),
            P(),
            P(),
            P(),
            P(("row", "col"), None, None),
            P(("row", "col"), None, None),
        ),
        out_specs=(P("row", "col", None), P(("row", "col"), None, None)),
        check_vma=False,
    )
```
